32 devices in a mesh: group: 2 (over x), box: 8 (over z, y), sample: 2 (over core).
Axes of the slice: x: 2, y: 2, z: 4, core: 2. Of those that a mesh axis runs over, the one named last changes fastest.
Arguments:
- krylov: float32 [2, 4, 4, 96, 256], P(None, None, None, ('group', 'box', 'sample')), parts along dimension 3, as said below
- self_inv: bfloat16 [2, 96, 256, 256], P(None, ('group', 'box', 'sample')), parts along dimension 1
- node_pos: float32 [3, 96, 256], P(None, ('group', 'box', 'sample')), parts along dimension 1, as said below
- node_wts: float32 [96, 256], P(('group', 'box', 'sample')), parts along dimension 0, may hold values from 0.02 to 0.2
- box_of: int32 [96], P(('group', 'box', 'sample')), parts along dimension 0, may hold values from 0 to 31, as said below
- near_list: int32 [96, 4], P(('group', 'box', 'sample')), parts along dimension 0, may hold values from 0 to 47, as said below
- leaf_src: int32 [64, 4], P(('group', 'box', 'sample')), parts along dimension 0, may hold values from 0 to 31, as said below
- leaf_op: int32 [64, 4], P(('group', 'box', 'sample')), parts along dimension 0, may hold values from 0 to 159
- leaf_ops: float32 [160, 2, 512], replicated, may hold values from -5 to 5
- interp: float32 [512, 2048], replicated, may hold values from -0.25 to 0.25
- parent_centers: float32 [3, 16], P(None, ('group', 'box')), parts along dimension 1
- up_src: int32 [16, 6], P('group'), parts along dimension 0, may hold values from 0 to 7, as said below
- up_op: int32 [16, 6], P('group'), parts along dimension 0, may hold values from 0 to 159
- up_ops: float32 [160, 2, 2048], P(None, None, 'sample'), may hold values from -1.5 to 1.5
Outputs:
- h_column: float32 [2, 4, 8], P(None, None, 'group'), parts along dimension 2
- h_norm: float32 [8], P('group'), parts along dimension 0
- next_vector: float32 [2, 4, 48, 512], P(None, None, ('box', 'sample'), 'group'), parts along dimension 3
The draws below stay inside these ranges and needn't reach their ends.
There are 2 independent parts, one for each index of `group`. The reference program is written for one: setup_inputs(seed, part) draws one part's arguments, and reference() takes and returns one part's arrays. A program takes and returns all parts, laid end to end along the dimension named above; an argument that names none is the same for every part. Nothing has to cross between parts.
Inputs may be any that keep to these rules, and one draw needn't show every extreme that they name: `krylov`: for each incidence the 4 vectors are orthonormal under the inner product that is the mean of conj(a) b over all nodes. `box_of`: Non-decreasing; ellipsoid e lies in one of the boxes 2 * (e // 3) to 2 * (e // 3) + 1, each of which holds at least one ellipsoid. `near_list`: an entry of row e is another ellipsoid at most 3 indices away from e. `leaf_src`: an entry of row b is another leaf box at most 2 indices away from b. `up_src`: no row names its own coarse box. `node_pos`: nodes of different ellipsoids are at least 0.2 apart.
All inputs are finite; a program needn't handle non-finite values.
Results may differ from the reference program's by a relative error of at most 0.0034.
Values sent between devices are 32-bit elements; how exact they have to be, the bound alone decides.
A program may use at most 64 MiB of HBM per device.

```python
import math
import jax
import jax.numpy as jnp
from jax import lax

NODES = 256
INC = 4
K_LEAF = 512
K_UP = 2048
OPS_LEAF = 160
OPS_UP = 160
ELL_DEV = 3
BOX_DEV = 2
MPREV = 4
NEAR = 4
FAR_LEAF = 4
FAR_UP = 6
ELLS = 48
BOXES = 32
PARENTS = 8


def draw_krylov(key, part):
    rows_all = ELLS * NODES
    parts_drawn = jax.random.normal(key, (2, INC, rows_all, MPREV), jnp.float32)
    matrix = lax.complex(parts_drawn[0], parts_drawn[1])
    basis = jnp.linalg.qr(matrix)[0] * jnp.sqrt(jnp.float32(rows_all))
    real_part = jnp.transpose(jnp.real(basis), (2, 0, 1)).reshape(MPREV, INC, ELLS, NODES)
    imag_part = jnp.transpose(jnp.imag(basis), (2, 0, 1)).reshape(MPREV, INC, ELLS, NODES)
    return jnp.stack([real_part, imag_part]).astype(jnp.float32)


def draw_self_inv(key, part):
    first_key = jax.random.fold_in(jax.random.fold_in(key, 3), 0)
    noise = jax.random.normal(first_key, (2, ELLS, NODES, NODES), jnp.float32) * (0.6 / NODES ** 0.5)
    identity = jnp.eye(NODES, dtype=jnp.float32)
    return jnp.stack([identity[None] + noise[0], noise[1]]).astype(jnp.bfloat16)


def draw_node_pos(key, part):
    first_key, second_key, third_key = jax.random.split(jax.random.fold_in(key, 5), 3)
    along = 1.2 * jnp.arange(ELLS).astype(jnp.float32)
    across = jax.random.uniform(first_key, (2, ELLS), jnp.float32, -0.3, 0.3)
    center = jnp.concatenate([along[None], across], axis=0)
    semi_axes = jax.random.uniform(second_key, (3, ELLS), jnp.float32, 0.2, 0.5)
    heading = jax.random.normal(third_key, (3, ELLS, NODES), jnp.float32)
    heading = heading / jnp.sqrt(jnp.sum(heading * heading, axis=0, keepdims=True) + 1e-12)
    return center[:, :, None] + semi_axes[:, :, None] * heading


def draw_box_of(key, part):
    devices = ELLS // ELL_DEV
    keys = jax.random.split(jax.random.fold_in(key, 7), devices)

    def one_device(dev_key):
        order = jax.random.permutation(dev_key, ELL_DEV - 1) + 1
        cuts = order[:BOX_DEV - 1]
        places = jnp.arange(ELL_DEV)
        return jnp.sum((places[:, None] >= cuts[None, :]).astype(jnp.int32), axis=1)
    local_ids = jax.vmap(one_device)(keys)
    return (local_ids + (jnp.arange(devices) * BOX_DEV)[:, None]).reshape(-1).astype(jnp.int32)


def nearby_indices(key, amount, reach, columns):
    first_key, second_key = jax.random.split(key, 2)
    stride = jax.random.randint(first_key, (amount, columns), 1, reach + 1)
    direction = jax.random.randint(second_key, (amount, columns), 0, 2) * 2 - 1
    itself = jnp.arange(amount)[:, None]
    forward = itself + direction * stride
    backward = itself - direction * stride
    return jnp.where((forward < 0) | (forward >= amount), backward, forward).astype(jnp.int32)


def draw_near_list(key, part):
    return nearby_indices(jax.random.fold_in(key, 11), ELLS, ELL_DEV, NEAR)


def draw_leaf_src(key, part):
    return nearby_indices(jax.random.fold_in(key, 13), BOXES, BOX_DEV, FAR_LEAF)


def draw_up_src(key, part):
    jumps = jax.random.randint(jax.random.fold_in(key, 17), (PARENTS, FAR_UP), 1, PARENTS)
    return ((jnp.arange(PARENTS)[:, None] + jumps) % PARENTS).astype(jnp.int32)


def draw_parent_centers(key, part):
    first_key, second_key = jax.random.split(jax.random.fold_in(key, 19), 2)
    per_parent = ELLS // PARENTS
    middle = 1.2 * (jnp.arange(PARENTS).astype(jnp.float32) * per_parent + (per_parent - 1) / 2.0)
    along = middle + jax.random.uniform(first_key, (PARENTS,), jnp.float32, -0.5, 0.5)
    across = jax.random.uniform(second_key, (2, PARENTS), jnp.float32, -0.3, 0.3)
    return jnp.concatenate([along[None], across], axis=0)


def set_ends(array, rng, smallest, largest):
    longest = array.shape.index(max(array.shape))
    spots = []
    for shift in (0, 1):
        where = [jax.random.randint(jax.random.fold_in(rng, axis), (), 0, length) for axis, length in enumerate(array.shape)]
        where[longest] = (where[longest] + shift) % array.shape[longest]
        spots.append(tuple(where))
    return array.at[spots[0]].set(smallest).at[spots[1]].set(largest)


def block_levels(rng, extent, cuts, least, largest):
    level = 1.0
    for dim, shards_of in cuts:
        draws = jax.random.uniform(jax.random.fold_in(jax.random.fold_in(rng, 6), dim), (shards_of,), jnp.float32, least / len(cuts), largest / len(cuts))
        level = level * jnp.repeat(jnp.exp(draws), extent[dim] // shards_of).reshape((-1,) + (1,) * (len(extent) - 1 - dim))
    return level


def scatter_about(stream_key, shape, scale, most, pieces=(), held_as=jnp.bfloat16):
    values = jax.random.normal(stream_key, shape, jnp.float32) * scale
    if len(pieces) > 0:
        values = block_levels(stream_key, shape, pieces, -0.22, 0.18) * values
    return jnp.clip(values, min=-most, max=most).astype(held_as)


def setup_inputs(seed: int = 0, part: int = 0) -> dict:
    seeds = jax.random.split(jax.random.key(seed), 15)
    own_keys = jax.random.split(jax.random.fold_in(seeds[14], part), 15)
    return {
        "krylov": draw_krylov(jax.random.fold_in(jax.random.fold_in(seeds[14], part), 71), part),
        "self_inv": draw_self_inv(jax.random.fold_in(jax.random.fold_in(seeds[14], part), 71), part),
        "node_pos": draw_node_pos(jax.random.fold_in(jax.random.fold_in(seeds[14], part), 71), part),
        "node_wts": jnp.clip(jnp.exp(math.log(0.2) - 2.3025851 * jax.random.uniform(own_keys[3], (ELLS, NODES), jnp.float32) ** block_levels(own_keys[3], (ELLS, NODES), ((0, 16),), -0.2, 0.2)), 0.02, 0.2),
        "box_of": draw_box_of(jax.random.fold_in(jax.random.fold_in(seeds[14], part), 71), part),
        "near_list": draw_near_list(jax.random.fold_in(jax.random.fold_in(seeds[14], part), 71), part),
        "leaf_src": draw_leaf_src(jax.random.fold_in(jax.random.fold_in(seeds[14], part), 71), part),
        "leaf_op": set_ends(jax.random.randint(own_keys[7], (BOXES, FAR_LEAF), 0, OPS_LEAF), jax.random.fold_in(own_keys[7], 1), 0, OPS_LEAF - 1).astype(jnp.int32),
        "leaf_ops": scatter_about(seeds[8], (OPS_LEAF, 2, K_LEAF), 0.35, 5.0, (), jnp.float32),
        "interp": scatter_about(seeds[9], (K_LEAF, K_UP), K_LEAF ** -0.5, 0.25, (), jnp.float32),
        "parent_centers": draw_parent_centers(jax.random.fold_in(jax.random.fold_in(seeds[14], part), 71), part),
        "up_src": draw_up_src(jax.random.fold_in(jax.random.fold_in(seeds[14], part), 71), part),
        "up_op": set_ends(jax.random.randint(own_keys[12], (PARENTS, FAR_UP), 0, OPS_UP), jax.random.fold_in(own_keys[12], 1), 0, OPS_UP - 1).astype(jnp.int32),
        "up_ops": scatter_about(seeds[13], (OPS_UP, 2, K_UP), 0.1, 1.5, ((2, 2),), jnp.float32),
    }


highest = lax.Precision.HIGHEST
wave_number = 2.0 * math.pi
golden_angle = math.pi * (3.0 - math.sqrt(5.0))

def sphere_points(amount, first_index, total_points):
    position = (first_index + jnp.arange(amount)).astype(jnp.float32)
    height = 1.0 - (2.0 * position + 1.0) / total_points
    radius = jnp.sqrt(1.0 - height * height)
    angle = position * golden_angle
    return jnp.stack([radius * jnp.cos(angle), radius * jnp.sin(angle), height])

def near_field(target, source_pos, source_val):
    squared = jnp.zeros((source_pos.shape[1], target.shape[1], source_pos.shape[2]), jnp.float32)
    for axis_index in range(3):
        spacing = target[axis_index][None, :, None] - source_pos[axis_index][:, None, :]
        squared = squared + spacing * spacing
    distance = jnp.sqrt(squared)
    kernel_real = jnp.cos(wave_number * distance) / distance
    kernel_imag = jnp.sin(wave_number * distance) / distance

    def contract(kernel, values):
        return jnp.einsum('jnm,ijm->in', kernel, values, precision=highest)
    return jnp.stack([contract(kernel_real, source_val[0]) - contract(kernel_imag, source_val[1]), contract(kernel_real, source_val[1]) + contract(kernel_imag, source_val[0])])

def translate(patterns, operators):
    op_real = operators[:, :, 0]
    op_imag = operators[:, :, 1]
    real_part = lax.optimization_barrier(jnp.sum(op_real * patterns[0] - op_imag * patterns[1], axis=2))
    imag_part = lax.optimization_barrier(jnp.sum(op_real * patterns[1] + op_imag * patterns[0], axis=2))
    return jnp.stack([real_part, imag_part])

def reference(krylov, self_inv, node_pos, node_wts, box_of, near_list, leaf_src, leaf_op, leaf_ops, interp, parent_centers, up_src, up_op, up_ops):
    vector = krylov[:, MPREV - 1]
    rounded = vector.astype(jnp.bfloat16)

    def invert(operands):
        block_pair, values = operands
        block_real = block_pair[0].astype(jnp.float32)
        block_imag = block_pair[1].astype(jnp.float32)
        val_real = values[0].astype(jnp.float32)
        val_imag = values[1].astype(jnp.float32)

        def times(matrix, vec_part):
            return jnp.dot(vec_part, matrix.T, precision=highest)
        return jnp.stack([times(block_real, val_real) - times(block_imag, val_imag), times(block_real, val_imag) + times(block_imag, val_real)])
    solved = jnp.moveaxis(lax.map(invert, (jnp.moveaxis(self_inv, 1, 0), jnp.moveaxis(rounded, 2, 0))), 0, 2)
    source = solved * node_wts[None, None]

    def near_one(operands):
        target, links = operands
        return near_field(target, node_pos[:, links], source[:, :, links])
    near = jnp.moveaxis(lax.map(near_one, (jnp.moveaxis(node_pos, 1, 0), near_list)), 0, 2)
    member = (box_of[None, :] == jnp.arange(BOXES)[:, None]).astype(jnp.float32)
    centers = jnp.dot(member, lax.optimization_barrier(jnp.sum(node_pos, axis=2)).T, precision=highest) / (lax.optimization_barrier(jnp.sum(member, axis=1)) * NODES)[:, None]
    ell_center = jnp.dot(member.T, centers, precision=highest)
    leaf_dirs = sphere_points(K_LEAF, 0, K_LEAF)

    def phases(position, center):
        angle = wave_number * jnp.dot(leaf_dirs.T, position - center[:, None], precision=highest)
        return (jnp.cos(angle), jnp.sin(angle))

    def aggregate(operands):
        position, center, values = operands
        cosine, sine = phases(position, center)
        real_part = jnp.dot(values[0], cosine.T, precision=highest) + jnp.dot(values[1], sine.T, precision=highest)
        imag_part = jnp.dot(values[1], cosine.T, precision=highest) - jnp.dot(values[0], sine.T, precision=highest)
        return jnp.stack([real_part, imag_part])
    moved_pos = jnp.moveaxis(node_pos, 1, 0)
    radiated = lax.map(aggregate, (moved_pos, ell_center, jnp.moveaxis(source, 2, 0)))
    patterns = jnp.einsum('be,eqik->qibk', member, radiated, precision=highest)
    leaf_in = translate(patterns[:, :, leaf_src], leaf_ops[leaf_op])
    parent_of = jnp.arange(BOXES) // (BOXES // PARENTS)
    up_dirs = sphere_points(K_UP, 0, K_UP)
    up_angle = wave_number * jnp.dot(centers - parent_centers[:, parent_of].T, up_dirs, precision=highest)
    up_cos = jnp.cos(up_angle)
    up_sin = jnp.sin(up_angle)
    lifted = jnp.einsum('qibk,kl->qibl', patterns, interp, precision=highest)
    shifted = jnp.stack([up_cos * lifted[0] + up_sin * lifted[1], up_cos * lifted[1] - up_sin * lifted[0]])
    parents = lax.optimization_barrier(jnp.sum(shifted.reshape(2, INC, PARENTS, BOXES // PARENTS, K_UP), axis=3))
    parent_in = translate(parents[:, :, up_src], up_ops[up_op])
    spread = parent_in[:, :, parent_of]
    lowered = jnp.stack([up_cos * spread[0] - up_sin * spread[1], up_cos * spread[1] + up_sin * spread[0]])
    incoming = leaf_in + jnp.einsum('qibl,kl->qibk', lowered, interp, precision=highest)

    def receive(operands):
        position, center, arriving = operands
        cosine, sine = phases(position, center)
        real_part = jnp.dot(arriving[0], cosine, precision=highest) - jnp.dot(arriving[1], sine, precision=highest)
        imag_part = jnp.dot(arriving[1], cosine, precision=highest) + jnp.dot(arriving[0], sine, precision=highest)
        return jnp.stack([real_part, imag_part]) * K_LEAF ** (-0.5)
    far = jnp.moveaxis(lax.map(receive, (moved_pos, ell_center, jnp.moveaxis(incoming[:, :, box_of], 2, 0))), 0, 2)
    result = vector + near + far
    unknowns = ELLS * NODES
    dot_real = lax.optimization_barrier(jnp.sum(krylov[0] * result[0][None] + krylov[1] * result[1][None], axis=(2, 3)))
    dot_imag = lax.optimization_barrier(jnp.sum(krylov[0] * result[1][None] - krylov[1] * result[0][None], axis=(2, 3)))
    proj_real = dot_real / unknowns
    proj_imag = dot_imag / unknowns
    weight_real = proj_real[:, :, None, None]
    weight_imag = proj_imag[:, :, None, None]
    kept_real = result[0] - lax.optimization_barrier(jnp.sum(weight_real * krylov[0] - weight_imag * krylov[1], axis=0))
    kept_imag = result[1] - lax.optimization_barrier(jnp.sum(weight_real * krylov[1] + weight_imag * krylov[0], axis=0))
    norm_sq = lax.optimization_barrier(jnp.sum(kept_real * kept_real + kept_imag * kept_imag, axis=(1, 2))) / unknowns
    h_norm = jnp.sqrt(norm_sq)
    next_vector = jnp.stack([kept_real, kept_imag]) / h_norm[None, :, None, None]
    return (jnp.stack([proj_real, proj_imag]), h_norm, next_vector)
```

```python
import functools
import math

import jax
import jax.numpy as jnp
import numpy as np
from jax import lax
from jax.experimental import pallas as pl
from jax.experimental.pallas import tpu as pltpu
from jax.sharding import PartitionSpec as P

MESH = pl.DeviceIdType.MESH
F32 = jnp.float32
BF16 = jnp.bfloat16
ROWS = 64
SPAN = 128
SPLITS = ((0, 0), (1, 0), (2, 0), (0, 1), (1, 1), (0, 2))


def sphere_points(total):
    position = np.arange(total).astype(np.float32)
    height = np.float32(1.0) - (np.float32(2.0) * position + np.float32(1.0)) / np.float32(total)
    radius = np.sqrt(np.float32(1.0) - height * height)
    angle = (position * np.float32(math.pi * (3.0 - math.sqrt(5.0)))).astype(np.float64)
    points = [radius * np.cos(angle).astype(np.float32), radius * np.sin(angle).astype(np.float32), height]
    return np.stack(points).astype(np.float32)


SIN_TABLE = (4.44286798223381, -7.307445412162602, 3.594802094687321, -0.7844036018968589)
COS_TABLE = (1.414204080580398, -6.977642059296966, 5.715238406047747, -1.7283486673722932)
SIN_FULL = (4.442882834891658, -7.308241184631927, 3.6062893308970487, -0.8457654001243101, 0.10920874958601288)
COS_FULL = (1.4142134965660362, -6.978850988281385, 5.739461171112273, -1.88356298861798, 0.31069819238699753)


def series(coefs, u):
    total = coefs[-1]
    for coef in coefs[-2::-1]:
        total = total * u + coef
    return total


def half_turn(t, sin_coefs, cos_coefs):
    f = t - jnp.round(t)
    u = f * f
    return series(sin_coefs, u) * f, series(cos_coefs, u)


def turn(t, sin_coefs=SIN_TABLE, cos_coefs=COS_TABLE):
    s, c = half_turn(t, sin_coefs, cos_coefs)
    return 1.0 - s * s, s * c


def thirds(x):
    high = x.astype(BF16).astype(F32)
    rest = x - high
    middle = rest.astype(BF16).astype(F32)
    return high, middle, rest - middle


def pair(x):
    high = x.astype(BF16).astype(F32)
    return jnp.concatenate([high, x - high], axis=0).astype(BF16)


def both(x, table, contract):
    rows = x.shape[0]
    out = lax.dot_general(
        pair(x), table, (((1,), (contract,)), ((), ())), preferred_element_type=F32
    )
    return out[:rows] + out[rows:]


def kernel(
    box_count_axis,
    sample_count_axis,
    box_of_hbm,
    near_list_hbm,
    leaf_src_hbm,
    leaf_op_hbm,
    up_src_hbm,
    up_op_hbm,
    parent_centers_hbm,
    krylov_hbm,
    self_inv_hbm,
    node_pos_hbm,
    node_wts_hbm,
    leaf_dirs_hbm,
    up_dirs_hbm,
    leaf_ops_hbm,
    interp_hbm,
    up_ops_hbm,
    h_out,
    norm_out,
    next_out,
    box_of,
    near_list,
    leaf_src,
    leaf_op,
    up_src,
    up_op,
    parent_centers,
    krylov,
    self_inv,
    node_pos,
    node_wts,
    leaf_dirs,
    up_dirs,
    leaf_ops,
    interp_raw,
    up_ops,
    interp,
    ks,
    halo,
    phases,
    columns,
    split_pos,
    cos_tab,
    sin_tab,
    pat,
    give,
    take,
    gathered,
    full,
    near_r,
    near_i,
    near_acc,
    result,
    sums,
    local_sem,
    send_a,
    recv_a,
    send_b,
    recv_b,
    send_c,
    recv_c,
    send_d,
    recv_d,
    send_e,
    recv_e,
    send_f,
    recv_f,
):
    nb, ns = box_count_axis, sample_count_axis
    nd = nb * ns
    _, vectors, ells, inc, nodes = krylov.shape
    rows = 2 * inc
    boxes = leaf_src.shape[0]
    near_count = near_list.shape[1]
    leaf_width = interp.shape[1]
    half = interp.shape[2]
    pairs_total = ells * near_count
    bi = lax.axis_index("box")
    si = lax.axis_index("sample")
    dev = bi * ns + si

    def load(slot, source, target):
        copy = pltpu.make_async_copy(source, target, local_sem.at[slot])
        copy.start()
        return copy

    loads = {}
    arrays = dict(
        node_pos=(node_pos_hbm, node_pos), box_of=(box_of_hbm, box_of), leaf_dirs=(leaf_dirs_hbm, leaf_dirs),
        krylov=(krylov_hbm, krylov), node_wts=(node_wts_hbm, node_wts), self_inv=(self_inv_hbm, self_inv),
        parent_centers=(parent_centers_hbm, parent_centers), up_dirs=(up_dirs_hbm, up_dirs),
        near_list=(near_list_hbm, near_list), leaf_src=(leaf_src_hbm, leaf_src), leaf_op=(leaf_op_hbm, leaf_op),
        up_src=(up_src_hbm, up_src), up_op=(up_op_hbm, up_op),
    )
    for name, (source, target) in arrays.items():
        loads[name] = load(len(loads), source, target)
    for h in range(ns):
        loads["interp", h] = load(len(loads), interp_hbm.at[:, pl.ds(h * half, half)], interp_raw.at[h])
    loads["up_ops"] = load(len(loads), up_ops_hbm, up_ops)
    loads["leaf_ops"] = load(len(loads), leaf_ops_hbm, leaf_ops)

    def ready(*wanted):
        for name in wanted:
            loads[name].wait()

    def place(index):
        return {"box": index // ns, "sample": index % ns}

    barrier = pltpu.get_barrier_semaphore()
    for off in range(1, nd):
        pl.semaphore_signal(barrier, inc=1, device_id=place((dev + off) % nd), device_id_type=MESH)

    sign = jnp.where(lax.broadcasted_iota(jnp.int32, (rows, 1), 0) < inc, 1.0, -1.0)

    def swap(x):
        return pltpu.roll(x, inc, 0)

    def inward(c, d):
        return c - sign * swap(d)

    def outward(c, d):
        return c + sign * swap(d)

    def neighbours(buffer, width, send, recv):
        own = buffer.at[pl.ds(width, width)]
        right = pltpu.make_async_remote_copy(
            src_ref=own, dst_ref=buffer.at[pl.ds(0, width)], send_sem=send.at[0], recv_sem=recv.at[0],
            device_id=place((dev + 1) % nd), device_id_type=MESH,
        )
        left = pltpu.make_async_remote_copy(
            src_ref=own, dst_ref=buffer.at[pl.ds(2 * width, width)], send_sem=send.at[1], recv_sem=recv.at[1],
            device_id=place((dev + nd - 1) % nd), device_id_type=MESH,
        )

        def start():
            @pl.when(dev < nd - 1)
            def _():
                right.start()

            @pl.when(dev > 0)
            def _():
                left.start()

        def arrive():
            @pl.when(dev > 0)
            def _():
                right.wait_recv()

            @pl.when(dev < nd - 1)
            def _():
                left.wait_recv()

        def finish():
            @pl.when(dev < nd - 1)
            def _():
                right.wait_send()

            @pl.when(dev > 0)
            def _():
                left.wait_send()

        return start, arrive, finish

    start_a, arrive_a, finish_a = neighbours(halo, ells, send_a, recv_a)
    start_b, arrive_b, finish_b = neighbours(pat, boxes, send_b, recv_b)

    ready("node_pos", "box_of", "leaf_dirs")
    for e in range(ells):
        for axis in range(3):
            halo[ells + e, rows + axis : rows + axis + 1, :] = node_pos[axis, e : e + 1, :]
        halo[ells + e, rows + 3 :, :] = jnp.zeros((halo.shape[1] - rows - 3, nodes), F32)

    member = [
        [jnp.where(box_of[e] - dev * boxes == b, 1.0, 0.0) for e in range(ells)] for b in range(boxes)
    ]
    position_sum = [
        jnp.sum(halo[ells + e, rows : rows + 8, :], axis=1, keepdims=True) for e in range(ells)
    ]
    centers = []
    for b in range(boxes):
        total = position_sum[0] * member[b][0]
        amount = member[b][0]
        for e in range(1, ells):
            total = total + position_sum[e] * member[b][e]
            amount = amount + member[b][e]
        centers.append(total / (jnp.full((8, 1), 1.0, F32) * (amount * nodes)))
    for e in range(ells):
        middle = centers[0] * member[0][e]
        for b in range(1, boxes):
            middle = middle + centers[b] * member[b][e]
        here = halo[ells + e, rows : rows + 8, :]
        pieces = thirds(here - middle)
        split_pos[e] = jnp.concatenate([pieces[p] for _, p in SPLITS], axis=0).astype(BF16)
        columns[e] = jnp.transpose(here)

    ready("krylov", "node_wts", "self_inv")
    for e in range(ells):
        for m in range(vectors):
            for q in range(2):
                ks[m, e, q * inc : (q + 1) * inc, :] = krylov[q, m, e]
    nt = (((1,), (1,)), ((), ()))
    halves_of_values = []
    for e in range(ells):
        rounded = ks[vectors - 1, e].astype(BF16)
        c = lax.dot_general(rounded, self_inv[0, e], nt, preferred_element_type=F32)
        d = lax.dot_general(rounded, self_inv[1, e], nt, preferred_element_type=F32)
        source = inward(c, d) * node_wts[e : e + 1, :]
        halo[ells + e, 0:rows, :] = source
        halves_of_values.append(pair(source))

    ready("parent_centers", "up_dirs")

    def up_phase(center, dirs):
        t = (center[0:1] - parent_centers[0, 0]) * dirs[0:1]
        for axis in range(1, 3):
            t = t + (center[axis : axis + 1] - parent_centers[0, axis]) * dirs[axis : axis + 1]
        return t

    def turns_of(list_of_centers, dirs):
        t = jnp.concatenate([up_phase(center, dirs) for center in list_of_centers], axis=0)
        return turn(t, SIN_FULL, COS_FULL)

    halves = (si, (si + 1) % ns)
    for slot, h in enumerate(halves):
        cosine, sine = turns_of(centers, up_dirs[h])
        phases[slot, 0] = cosine
        phases[slot, 1] = sine

    for start in range(0, leaf_width, SPAN):
        span = pl.ds(start, SPAN)
        totals = [None] * boxes
        for e in range(ells):
            t = jnp.dot(leaf_dirs[span, :], split_pos[e], preferred_element_type=F32)
            cosine, sine = turn(t)
            cosine, sine = cosine.astype(BF16), sine.astype(BF16)
            cos_tab[e, span, :] = cosine
            sin_tab[e, span, :] = sine
            c = lax.dot_general(halves_of_values[e], cosine, nt, preferred_element_type=F32)
            d = lax.dot_general(halves_of_values[e], sine, nt, preferred_element_type=F32)
            piece = outward(c[:rows] + c[rows:], d[:rows] + d[rows:])
            for b in range(boxes):
                part = piece * member[b][e]
                totals[b] = part if e == 0 else totals[b] + part
        for b in range(boxes):
            pat[boxes + b, :, span] = totals[b]

    for h in range(ns):
        ready(("interp", h))
    whole = pair(jnp.concatenate([pat[boxes + b] for b in range(boxes)], axis=0))

    def lift(slot):
        table = interp_raw[halves[slot]].astype(BF16)
        interp[halves[slot]] = table
        lifted = jnp.dot(whole, table, preferred_element_type=F32)
        lifted = lifted[: boxes * rows] + lifted[boxes * rows :]
        parent = None
        for b in range(boxes):
            piece = lifted[b * rows : (b + 1) * rows]
            term = outward(
                piece * phases[slot, 0, b : b + 1, :], piece * phases[slot, 1, b : b + 1, :]
            )
            parent = term if parent is None else parent + term
        return parent

    give[...] = lift(1)
    partner_id = {"box": bi, "sample": (si + 1) % ns}
    swap_parts = pltpu.make_async_remote_copy(
        src_ref=give, dst_ref=take, send_sem=send_f.at[0], recv_sem=recv_f.at[0],
        device_id=partner_id, device_id_type=MESH,
    )
    pl.semaphore_wait(barrier, nd - 1)
    swap_parts.start()
    start_b()
    start_a()
    own_part = lift(0)
    swap_parts.wait_recv()
    gathered[bi] = own_part + take[...]

    def deliver(off, slot):
        return pltpu.make_async_remote_copy(
            src_ref=gathered.at[slot], dst_ref=gathered.at[slot], send_sem=send_c.at[off],
            recv_sem=recv_c.at[slot], device_id={"box": (bi + off) % nb, "sample": si}, device_id_type=MESH,
        )

    for off in range(1, nb):
        deliver(off, bi).start()

    def translate(operators, index, values):
        pair_rows = operators[index]
        return inward(values * pair_rows[0:1], values * pair_rows[1:2])

    ready("near_list")
    arrive_a()
    near_acc[...] = jnp.zeros(near_acc.shape, F32)

    def near_pair(index, slot):
        e = index // near_count
        j = index % near_count
        source = halo[jnp.clip(near_list[e, j] - (dev - 1) * ells, 0, 3 * ells - 1)]
        for chunk in range(nodes // ROWS):
            target = columns[e, chunk * ROWS : (chunk + 1) * ROWS, :]
            squared = None
            for axis in range(3):
                gap = target[:, axis : axis + 1] - source[rows + axis : rows + axis + 1]
                squared = gap * gap if squared is None else squared + gap * gap
            inverse = lax.rsqrt(squared)
            s, c = half_turn(squared * inverse, SIN_TABLE, COS_TABLE)
            scaled = s * inverse
            near_r[slot, chunk * ROWS : (chunk + 1) * ROWS, :] = (inverse - s * scaled).astype(BF16)
            near_i[slot, chunk * ROWS : (chunk + 1) * ROWS, :] = (scaled * c).astype(BF16)
        values = source[0:rows]
        near_acc[e] += inward(both(values, near_r[slot], 1), both(values, near_i[slot], 1))

    group = 2 if pairs_total % 2 == 0 else 1

    def near_group(index, carry):
        for slot in range(group):
            near_pair(index * group + slot, slot)
        return carry

    lax.fori_loop(0, pairs_total // group, near_group, 0)

    arrive_b()
    ready("leaf_src", "leaf_op", "leaf_ops")
    incoming = []
    for b in range(boxes):
        total = None
        for j in range(leaf_src.shape[1]):
            source = pat[jnp.clip(leaf_src[b, j] - (dev - 1) * boxes, 0, 3 * boxes - 1)]
            term = translate(leaf_ops, leaf_op[b, j], source)
            total = term if total is None else total + term
        incoming.append(total)


    ready("up_src", "up_op", "up_ops")
    for off in range(1, nb):
        deliver(off, (bi + off) % nb).wait_recv()
    parent_in = None
    for j in range(up_src.shape[1]):
        term = translate(up_ops, up_op[bi, j], gathered[up_src[bi, j]])
        parent_in = term if parent_in is None else parent_in + term
    full[si] = parent_in
    partner = pltpu.make_async_remote_copy(
        src_ref=full.at[si], dst_ref=full.at[si], send_sem=send_d.at[0], recv_sem=recv_d.at[0],
        device_id=partner_id, device_id_type=MESH,
    )
    partner.start()

    def lower(slot):
        h = halves[slot]
        values = full[h]
        lowered = jnp.concatenate(
            [
                inward(values * phases[slot, 0, b : b + 1, :], values * phases[slot, 1, b : b + 1, :])
                for b in range(boxes)
            ],
            axis=0,
        )
        return both(lowered, interp[h], 1)

    lowered = lower(0)
    partner.wait_recv()
    lowered = lowered + lower(1)
    for b in range(boxes):
        incoming[b] = incoming[b] + lowered[b * rows : (b + 1) * rows]

    lane = lax.broadcasted_iota(jnp.int32, (rows, 128), 1)
    row = lax.broadcasted_iota(jnp.int32, (rows, 128), 0)
    square = jnp.zeros((rows, 1), F32)
    straight = [jnp.zeros((rows, 1), F32) for _ in range(vectors)]
    crossed = [jnp.zeros((rows, 1), F32) for _ in range(vectors)]
    for e in range(ells):
        arriving = incoming[0] * member[0][e]
        for b in range(1, boxes):
            arriving = arriving + incoming[b] * member[b][e]
        far = inward(both(arriving, cos_tab[e], 0), both(arriving, sin_tab[e], 0))
        value = ks[vectors - 1, e] + near_acc[e] + far * leaf_width ** (-0.5)
        result[e] = value
        other = swap(value)
        square = square + jnp.sum(value * value, axis=1, keepdims=True)
        for m in range(vectors):
            basis = ks[m, e]
            straight[m] = straight[m] + jnp.sum(basis * value, axis=1, keepdims=True)
            crossed[m] = crossed[m] + jnp.sum(basis * other, axis=1, keepdims=True)
    packed = jnp.where(lane == vectors * rows + row, jnp.broadcast_to(square, lane.shape), 0.0)
    for m in range(vectors):
        a = jnp.broadcast_to(straight[m], lane.shape)
        b = jnp.broadcast_to(crossed[m], lane.shape)
        dots = jnp.where(row < inc, a + swap(a), swap(b) - b)
        packed = packed + jnp.where(lane == m * rows + row, dots, 0.0)
    sums[dev] = jnp.sum(packed, axis=0, keepdims=True)
    for off in range(1, nd):
        pltpu.make_async_remote_copy(
            src_ref=sums.at[dev], dst_ref=sums.at[dev], send_sem=send_e.at[off], recv_sem=recv_e.at[dev],
            device_id=place((dev + off) % nd), device_id_type=MESH,
        ).start()
    for off in range(1, nd):
        other = (dev + off) % nd
        pltpu.make_async_remote_copy(
            src_ref=sums.at[other], dst_ref=sums.at[other], send_sem=send_e.at[off],
            recv_sem=recv_e.at[other], device_id=place(other), device_id_type=MESH,
        ).wait_recv()
    total = sums[0]
    for index in range(1, nd):
        total = total + sums[index]
    total = total * (1.0 / (ells * nodes * nd))
    spread = jnp.broadcast_to(total, lane.shape)

    def column(start):
        return jnp.sum(
            jnp.where(lane == start + lax.rem(row, inc), spread, 0.0), axis=1, keepdims=True
        )

    real = [column(m * rows) for m in range(vectors)]
    imag = [column(m * rows + inc) for m in range(vectors)]
    norm_sq = column(vectors * rows) + column(vectors * rows + inc)
    for m in range(vectors):
        norm_sq = norm_sq - (real[m] * real[m] + imag[m] * imag[m])
    norm = jnp.sqrt(norm_sq)
    for m in range(vectors):
        for q in range(2):
            at = m * rows + q * inc
            h_out[q, m : m + 1, :] = total[:, at : at + inc]
    flat = jnp.sum(
        jnp.where((lane == row) & (row < inc), jnp.broadcast_to(norm, lane.shape), 0.0), axis=0, keepdims=True
    )
    norm_out[...] = flat[:, 0:inc]
    for e in range(ells):
        kept = result[e]
        for m in range(vectors):
            basis = ks[m, e]
            kept = kept - inward(basis * real[m], basis * imag[m])
        kept = kept / norm
        for q in range(2):
            next_out[q, e] = kept[q * inc : (q + 1) * inc]

    finish_a()
    finish_b()
    partner.wait_send()
    swap_parts.wait_send()
    for off in range(1, nb):
        deliver(off, bi).wait_send()
    for off in range(1, nd):
        pltpu.make_async_remote_copy(
            src_ref=sums.at[dev], dst_ref=sums.at[dev], send_sem=send_e.at[off], recv_sem=recv_e.at[dev],
            device_id=place((dev + off) % nd), device_id_type=MESH,
        ).wait_send()


def hand_on(h_in, norm_in, next_in, h_out, norm_out, next_out):
    h_out[...] = h_in[...]
    norm_out[...] = norm_in[...]
    next_out[...] = next_in[...]


def body(
    nb,
    ns,
    krylov,
    self_inv,
    node_pos,
    node_wts,
    box_of,
    near_list,
    leaf_src,
    leaf_op,
    leaf_ops,
    interp,
    parent_centers,
    up_src,
    up_op,
    up_ops,
):
    _, vectors, inc, ells, nodes = krylov.shape
    rows = 2 * inc
    boxes = leaf_src.shape[0]
    leaf_width, up_width = interp.shape
    half = up_ops.shape[2]
    nd = nb * ns
    directions = sphere_points(leaf_width).T
    pieces = []
    for _ in range(3):
        pieces.append(directions.astype(BF16))
        directions = directions - pieces[-1].astype(np.float32)
    leaf_dirs = np.zeros((leaf_width, 8 * len(SPLITS)), BF16)
    for block, (piece, _) in enumerate(SPLITS):
        leaf_dirs[:, 8 * block : 8 * block + 3] = pieces[piece]
    up_dirs = np.zeros((ns, 8, half), np.float32)
    up_dirs[:, :3] = np.moveaxis(sphere_points(up_width).reshape(3, ns, half), 1, 0)
    small = [box_of, near_list, leaf_src, leaf_op, up_src, up_op, parent_centers.T]
    large = [jnp.transpose(krylov, (0, 1, 3, 2, 4)), self_inv, node_pos, node_wts]
    large += [jnp.asarray(leaf_dirs), jnp.asarray(up_dirs)]
    vmem = pl.BlockSpec(memory_space=pltpu.VMEM)
    hbm = pl.BlockSpec(memory_space=pl.ANY)
    dma = pltpu.SemaphoreType.DMA
    h_column, h_norm, next_vector = pl.pallas_call(
        functools.partial(kernel, nb, ns),
        out_shape=(
            jax.ShapeDtypeStruct((2, vectors, inc), F32),
            jax.ShapeDtypeStruct((1, inc), F32),
            jax.ShapeDtypeStruct((2, ells, inc, nodes), F32),
        ),
        in_specs=[hbm] * 16,
        out_specs=(vmem, vmem, vmem),
        scratch_shapes=[pltpu.SMEM(x.shape, x.dtype) for x in small]
        + [pltpu.VMEM(x.shape, x.dtype) for x in large]
        + [
            pltpu.VMEM(leaf_ops.shape, F32),
            pltpu.VMEM((ns, leaf_width, half), F32),
            pltpu.VMEM(up_ops.shape, F32),
            pltpu.VMEM((ns, leaf_width, half), BF16),
            pltpu.VMEM((vectors, ells, rows, nodes), F32),
            pltpu.VMEM((3 * ells, rows + 8, nodes), F32),
            pltpu.VMEM((ns, 2, boxes, half), F32),
            pltpu.VMEM((ells, nodes, 8), F32),
            pltpu.VMEM((ells, 8 * len(SPLITS), nodes), BF16),
            pltpu.VMEM((ells, leaf_width, nodes), BF16),
            pltpu.VMEM((ells, leaf_width, nodes), BF16),
            pltpu.VMEM((3 * boxes, rows, leaf_width), F32),
            pltpu.VMEM((rows, half), F32),
            pltpu.VMEM((rows, half), F32),
            pltpu.VMEM((nb, rows, half), F32),
            pltpu.VMEM((ns, rows, half), F32),
            pltpu.VMEM((2, nodes, nodes), BF16),
            pltpu.VMEM((2, nodes, nodes), BF16),
            pltpu.VMEM((ells, rows, nodes), F32),
            pltpu.VMEM((ells, rows, nodes), F32),
            pltpu.VMEM((nd, 1, 128), F32),
            dma((ns + 15,)),
            dma((2,)),
            dma((2,)),
            dma((2,)),
            dma((2,)),
            dma((nb,)),
            dma((nb,)),
            dma((1,)),
            dma((1,)),
            dma((nd,)),
            dma((nd,)),
            dma((1,)),
            dma((1,)),
        ],
        compiler_params=pltpu.CompilerParams(
            collective_id=0, has_side_effects=True, vmem_limit_bytes=67043328
        ),
    )(*small, *large, leaf_ops, interp, up_ops)
    h_column, h_norm, next_vector = pl.pallas_call(
        hand_on,
        out_shape=tuple(jax.ShapeDtypeStruct(x.shape, F32) for x in (h_column, h_norm, next_vector)),
        in_specs=[vmem] * 3,
        out_specs=(vmem, vmem, vmem),
    )(h_column, h_norm, next_vector)
    return h_column, h_norm.reshape(inc), jnp.transpose(next_vector, (0, 2, 1, 3))


def solution(mesh):
    placed = (
        P(None, None, None, ("group", "box", "sample"), None),
        P(None, ("group", "box", "sample"), None, None),
        P(None, ("group", "box", "sample"), None),
        P(("group", "box", "sample"), None),
        P(("group", "box", "sample")),
        P(("group", "box", "sample"), None),
        P(("group", "box", "sample"), None),
        P(("group", "box", "sample"), None),
        P(),
        P(),
        P(None, ("group", "box")),
        P("group", None),
        P("group", None),
        P(None, None, "sample"),
    )
    return jax.shard_map(
        functools.partial(body, mesh.shape["box"], mesh.shape["sample"]),
        mesh=mesh,
        in_specs=placed,
        out_specs=(P(None, None, "group"), P("group"), P(None, None, ("box", "sample"), "group")),
        check_vma=False,
    )
```

```python
import functools
import math

import jax
import jax.numpy as jnp
import numpy as np
from jax import lax
from jax.experimental import pallas as pl
from jax.experimental.pallas import tpu as pltpu
from jax.sharding import PartitionSpec as P

MESH = pl.DeviceIdType.MESH
F32 = jnp.float32
BF16 = jnp.bfloat16
ROWS = 64
SPAN = 128
SPLITS = ((0, 0), (1, 0), (2, 0), (0, 1), (1, 1), (0, 2))


def sphere_points(total):
    position = np.arange(total).astype(np.float32)
    height = np.float32(1.0) - (np.float32(2.0) * position + np.float32(1.0)) / np.float32(total)
    radius = np.sqrt(np.float32(1.0) - height * height)
    angle = (position * np.float32(math.pi * (3.0 - math.sqrt(5.0)))).astype(np.float64)
    points = [radius * np.cos(angle).astype(np.float32), radius * np.sin(angle).astype(np.float32), height]
    return np.stack(points).astype(np.float32)


SIN_TABLE = (4.44286798223381, -7.307445412162602, 3.594802094687321, -0.7844036018968589)
COS_TABLE = (1.414204080580398, -6.977642059296966, 5.715238406047747, -1.7283486673722932)
SIN_FULL = (4.442882834891658, -7.308241184631927, 3.6062893308970487, -0.8457654001243101, 0.10920874958601288)
COS_FULL = (1.4142134965660362, -6.978850988281385, 5.739461171112273, -1.88356298861798, 0.31069819238699753)


def series(coefs, u):
    total = coefs[-1]
    for coef in coefs[-2::-1]:
        total = total * u + coef
    return total


def half_turn(t, sin_coefs, cos_coefs):
    f = t - jnp.round(t)
    u = f * f
    return series(sin_coefs, u) * f, series(cos_coefs, u)


def turn(t, sin_coefs=SIN_TABLE, cos_coefs=COS_TABLE):
    s, c = half_turn(t, sin_coefs, cos_coefs)
    return 1.0 - s * s, s * c


def thirds(x):
    high = x.astype(BF16).astype(F32)
    rest = x - high
    middle = rest.astype(BF16).astype(F32)
    return high, middle, rest - middle


def pair(x):
    high = x.astype(BF16).astype(F32)
    return jnp.concatenate([high, x - high], axis=0).astype(BF16)


def both(x, table, contract):
    rows = x.shape[0]
    out = lax.dot_general(
        pair(x), table, (((1,), (contract,)), ((), ())), preferred_element_type=F32
    )
    return out[:rows] + out[rows:]


def kernel(
    box_count_axis,
    sample_count_axis,
    box_of_hbm,
    near_list_hbm,
    leaf_src_hbm,
    leaf_op_hbm,
    up_src_hbm,
    up_op_hbm,
    parent_centers_hbm,
    krylov_hbm,
    self_inv_hbm,
    node_pos_hbm,
    node_wts_hbm,
    leaf_dirs_hbm,
    up_dirs_hbm,
    leaf_ops_hbm,
    interp_hbm,
    up_ops_hbm,
    small_hbm,
    next_hbm,
    box_of,
    near_list,
    leaf_src,
    leaf_op,
    up_src,
    up_op,
    parent_centers,
    krylov,
    self_inv,
    node_pos,
    node_wts,
    leaf_dirs,
    up_dirs,
    leaf_ops,
    interp_raw,
    up_ops,
    interp,
    ks,
    halo,
    phases,
    columns,
    split_pos,
    turns,
    cos_tab,
    sin_tab,
    pat,
    give,
    take,
    parents,
    gathered,
    cross,
    full,
    squares,
    near_r,
    near_i,
    near_acc,
    result,
    sums,
    local_sem,
    recv_a,
    recv_b,
    recv_sem,
    small_out,
    next_out,
):
    nb, ns = box_count_axis, sample_count_axis
    nd = nb * ns
    _, vectors, ells, inc, nodes = krylov.shape
    rows = 2 * inc
    boxes = leaf_src.shape[0]
    near_count = near_list.shape[1]
    twins, leaf_width, part = interp.shape[1:]
    half = twins * part
    pairs_total = ells * near_count
    bi = lax.axis_index("box")
    si = lax.axis_index("sample")
    dev = bi * ns + si
    levels = nb // twins
    level = bi // twins
    twin = bi % twins

    def load(slot, source, target):
        copy = pltpu.make_async_copy(source, target, local_sem.at[slot])
        copy.start()
        return copy

    loads = {}

    def begin(**arrays):
        for name, (source, target) in arrays.items():
            loads[name] = load(len(loads), source, target)

    def ready(*wanted):
        for name in wanted:
            loads[name].wait()

    def place(index):
        return {"box": index // ns, "sample": index % ns}

    begin(node_pos=(node_pos_hbm, node_pos), box_of=(box_of_hbm, box_of), leaf_dirs=(leaf_dirs_hbm, leaf_dirs))
    barrier = pltpu.get_barrier_semaphore()
    for off in range(1, nd):
        pl.semaphore_signal(barrier, inc=1, device_id=place((dev + off) % nd), device_id_type=MESH)
    begin(
        krylov=(krylov_hbm, krylov), node_wts=(node_wts_hbm, node_wts), self_inv=(self_inv_hbm, self_inv),
        parent_centers=(parent_centers_hbm, parent_centers), up_dirs=(up_dirs_hbm, up_dirs),
    )
    halves = (si, (si + 1) % ns)
    for slot in range(ns - 1, -1, -1):
        at = pl.ds(pl.multiple_of(halves[slot] * half, half), half)
        loads["interp", slot] = load(len(loads), interp_hbm.at[:, at], interp_raw.at[slot])
    begin(
        near_list=(near_list_hbm, near_list), leaf_src=(leaf_src_hbm, leaf_src), leaf_op=(leaf_op_hbm, leaf_op),
        up_src=(up_src_hbm, up_src), up_op=(up_op_hbm, up_op), up_ops=(up_ops_hbm.at[:, :, pl.ds(pl.multiple_of(twin * part, part), part)], up_ops),
        leaf_ops=(leaf_ops_hbm, leaf_ops),
    )

    sign = jnp.where(lax.broadcasted_iota(jnp.int32, (rows, 1), 0) < inc, 1.0, -1.0)

    def swap(x):
        return pltpu.roll(x, inc, 0)

    def inward(c, d):
        return c - sign * swap(d)

    def outward(c, d):
        return c + sign * swap(d)

    def neighbours(buffer, width, send, recv):
        own = buffer.at[pl.ds(width, width)]
        right = pltpu.make_async_remote_copy(
            src_ref=own, dst_ref=buffer.at[pl.ds(0, width)], send_sem=local_sem.at[send], recv_sem=recv.at[0],
            device_id=place((dev + 1) % nd), device_id_type=MESH,
        )
        left = pltpu.make_async_remote_copy(
            src_ref=own, dst_ref=buffer.at[pl.ds(2 * width, width)], send_sem=local_sem.at[send + 1], recv_sem=recv.at[1],
            device_id=place((dev + nd - 1) % nd), device_id_type=MESH,
        )

        def start():
            @pl.when(dev < nd - 1)
            def _():
                right.start()

            @pl.when(dev > 0)
            def _():
                left.start()

        def arrive():
            @pl.when(dev > 0)
            def _():
                right.wait_recv()

            @pl.when(dev < nd - 1)
            def _():
                left.wait_recv()

        def finish():
            @pl.when(dev < nd - 1)
            def _():
                right.wait_send()

            @pl.when(dev > 0)
            def _():
                left.wait_send()

        return start, arrive, finish

    start_a, arrive_a, finish_a = neighbours(halo, ells, 0, recv_a)
    start_b, arrive_b, finish_b = neighbours(pat, boxes, 2, recv_b)

    ready("node_pos", "box_of", "leaf_dirs")
    for e in range(ells):
        for axis in range(3):
            halo[ells + e, rows + axis : rows + axis + 1, :] = node_pos[axis, e : e + 1, :]
        halo[ells + e, rows + 3 :, :] = jnp.zeros((halo.shape[1] - rows - 3, nodes), F32)

    member = [
        [jnp.where(box_of[e] - dev * boxes == b, 1.0, 0.0) for e in range(ells)] for b in range(boxes)
    ]
    position_sum = [
        jnp.sum(halo[ells + e, rows : rows + 8, :], axis=1, keepdims=True) for e in range(ells)
    ]
    centers = []
    for b in range(boxes):
        total = position_sum[0] * member[b][0]
        amount = member[b][0]
        for e in range(1, ells):
            total = total + position_sum[e] * member[b][e]
            amount = amount + member[b][e]
        centers.append(total / (jnp.full((8, 1), 1.0, F32) * (amount * nodes)))
    for e in range(ells):
        middle = centers[0] * member[0][e]
        for b in range(1, boxes):
            middle = middle + centers[b] * member[b][e]
        here = halo[ells + e, rows : rows + 8, :]
        pieces = thirds(here - middle)
        split_pos[e] = jnp.concatenate([pieces[p] for _, p in SPLITS], axis=0).astype(BF16)

    nt = (((1,), (1,)), ((), ()))
    spans = [pl.ds(start, SPAN) for start in range(0, leaf_width, SPAN)]

    def angles(e, span):
        turns[e, span, :] = jnp.dot(leaf_dirs[span, :], split_pos[e], preferred_element_type=F32)

    def fill(e, span):
        cosine, sine = turn(turns[e, span, :])
        cos_tab[e, span, :] = cosine.astype(BF16)
        sin_tab[e, span, :] = sine.astype(BF16)

    def gather_up(e, span):
        c = lax.dot_general(pairs[e], cos_tab[e, span, :], nt, preferred_element_type=F32)
        d = lax.dot_general(pairs[e], sin_tab[e, span, :], nt, preferred_element_type=F32)
        piece = outward(c[:rows] + c[rows:], d[:rows] + d[rows:])
        for b in range(boxes):
            part = piece * member[b][e]
            pat[boxes + b, :, span] = part if e == 0 else pat[boxes + b, :, span] + part

    for span in spans:
        angles(0, span)
    for span in spans:
        if ells > 1:
            angles(1, span)
        fill(0, span)

    ready("krylov", "node_wts", "self_inv", "parent_centers", "up_dirs")
    pairs = []
    for e in range(ells):
        rounded = jnp.concatenate([krylov[q, vectors - 1, e] for q in range(2)], axis=0).astype(BF16)
        c = lax.dot_general(rounded, self_inv[0, e], nt, preferred_element_type=F32)
        d = lax.dot_general(rounded, self_inv[1, e], nt, preferred_element_type=F32)
        source = inward(c, d) * node_wts[e : e + 1, :]
        halo[ells + e, 0:rows, :] = source
        pairs.append(pair(source))


    def up_phase(center, dirs):
        t = (center[0:1] - parent_centers[0, 0]) * dirs[0:1]
        for axis in range(1, 3):
            t = t + (center[axis : axis + 1] - parent_centers[0, axis]) * dirs[axis : axis + 1]
        return t

    def turns_of(list_of_centers, dirs):
        t = jnp.concatenate([up_phase(center, dirs) for center in list_of_centers], axis=0)
        return turn(t, SIN_FULL, COS_FULL)

    for slot, h in enumerate(halves):
        cosine, sine = turns_of(centers, up_dirs[h])
        for t in range(twins):
            phases[slot, t, 0] = cosine[:, t * part : (t + 1) * part]
            phases[slot, t, 1] = sine[:, t * part : (t + 1) * part]

    pending = [(0, span) for span in spans] if ells > 1 else []
    for e in range(min(1, ells - 1), ells):
        for span in spans:
            if e + 1 < ells:
                angles(e + 1, span)
            if e > 0:
                fill(e, span)
            for _ in range(min(len(pending), 2 if e > 1 else 1)):
                gather_up(*pending.pop(0))
            pending.append((e, span))
    for item in pending:
        gather_up(*item)

    pl.semaphore_wait(barrier, nd - 1)
    start_a()
    whole = pair(jnp.concatenate([pat[boxes + b] for b in range(boxes)], axis=0))

    def lift(slot):
        ready(("interp", slot))
        parents = []
        for t in range(twins):
            table = interp_raw[slot, :, t * part : (t + 1) * part].astype(BF16)
            interp[slot, t] = table
            lifted = jnp.dot(whole, table, preferred_element_type=F32)
            lifted = lifted[: boxes * rows] + lifted[boxes * rows :]
            parent = None
            for b in range(boxes):
                piece = lifted[b * rows : (b + 1) * rows]
                term = outward(
                    piece * phases[slot, t, 0, b : b + 1, :], piece * phases[slot, t, 1, b : b + 1, :]
                )
                parent = term if parent is None else parent + term
            parents.append(parent)
        return parents

    for t, parent in enumerate(lift(1)):
        give[t] = parent
    partner_id = {"box": bi, "sample": (si + 1) % ns}
    swap_parts = pltpu.make_async_remote_copy(
        src_ref=give, dst_ref=take, send_sem=local_sem.at[4], recv_sem=recv_sem.at[0],
        device_id=partner_id, device_id_type=MESH,
    )
    swap_parts.start()
    own_part = lift(0)
    swap_parts.wait_recv()
    for t in range(twins):
        parents[t] = own_part[t] + take[t]

    def bulk(ref, send, receive):
        return pltpu.make_async_remote_copy(
            src_ref=ref, dst_ref=ref, send_sem=local_sem.at[send], recv_sem=recv_sem.at[receive],
            device_id=partner_id, device_id_type=MESH,
        )

    def deliver(box):
        pltpu.make_async_remote_copy(
            src_ref=parents.at[box % twins], dst_ref=gathered.at[bi], send_sem=local_sem.at[5],
            recv_sem=recv_sem.at[1], device_id={"box": box, "sample": si}, device_id_type=MESH,
        ).start()

    for distance in range(levels - 1, 0, -1):
        for there, up in ((level + distance < levels, 1), (level >= distance, -1)):
            @pl.when(there)
            def _(distance=distance, up=up):
                for turned in range(twins):
                    deliver((level + up * distance) * twins + (bi + turned) % twins)
    if twins > 1:
        deliver(level * twins + (bi + 1) % twins)
    every_parent = bulk(gathered.at[pl.ds(0, nb - 1)], 5, 1)
    gathered[bi] = parents[twin]
    start_b()

    def edge(x, first, ones):
        parts = thirds(jnp.sum(x * x, axis=0, keepdims=True))
        at = lax.broadcasted_iota(jnp.int32, x.shape, 0)
        block = jnp.where((at >= ones) & (at < ones + 3), 1.0, 0.0)
        for p in range(3):
            block = jnp.where(at == first + p, jnp.broadcast_to(parts[p], x.shape), block)
        return block

    for e in range(ells):
        x = halo[ells + e, rows : rows + 8, :] - position_sum[e] * (1.0 / nodes)
        pieces = thirds(-2.0 * x)
        blocks = [pieces[p] for p, _ in SPLITS] + [edge(x, 3, 0)]
        blocks.append(jnp.zeros_like(x))
        columns[e] = jnp.transpose(jnp.concatenate(blocks, axis=0)).astype(BF16)
        for m in range(vectors):
            for q in range(2):
                ks[m, e, q * inc : (q + 1) * inc, :] = krylov[q, m, e]

    def translate(operators, index, values):
        pair_rows = operators[index]
        return inward(values * pair_rows[0:1], values * pair_rows[1:2])

    ready("near_list")
    arrive_a()
    near_acc[...] = jnp.zeros(near_acc.shape, F32)

    near_items = [(e, j) for e in range(ells) for j in range(near_count)]

    def near_source(e, j):
        return halo[jnp.clip(near_list[e, j] - (dev - 1) * ells, 0, 3 * ells - 1)]

    def distances(index):
        e, j = near_items[index]
        y = near_source(e, j)[rows : rows + 8] - position_sum[e] * (1.0 / nodes)
        pieces = thirds(y)
        blocks = [pieces[p] for _, p in SPLITS] + [edge(y, 0, 3), jnp.zeros_like(y)]
        split = jnp.concatenate(blocks, axis=0).astype(BF16)
        for chunk in range(0, nodes, ROWS):
            squares[index % 2, chunk : chunk + ROWS, :] = jnp.dot(
                columns[e, chunk : chunk + ROWS, :], split, preferred_element_type=F32
            )

    def near_pair(index):
        e, j = near_items[index]
        slot = index % 2
        for chunk in range(0, nodes, ROWS):
            squared = squares[slot, chunk : chunk + ROWS, :]
            inverse = lax.rsqrt(squared)
            s, c = half_turn(squared * inverse, SIN_TABLE, COS_TABLE)
            scaled = s * inverse
            near_r[slot, chunk : chunk + ROWS, :] = (inverse - s * scaled).astype(BF16)
            near_i[slot, chunk : chunk + ROWS, :] = (scaled * c).astype(BF16)
        values = near_source(e, j)[0:rows]
        near_acc[e] += inward(both(values, near_r[slot], 1), both(values, near_i[slot], 1))

    distances(0)
    for index in range(pairs_total):
        if index + 1 < pairs_total:
            distances(index + 1)
        near_pair(index)

    ready("up_src", "up_op", "up_ops")
    every_parent.wait_recv()

    def coarse(box):
        total = None
        for j in range(up_src.shape[1]):
            term = translate(up_ops, up_op[box, j], gathered[up_src[box, j]])
            total = term if total is None else total + term
        return total

    def hand(source, receive, box, sample):
        pltpu.make_async_remote_copy(
            src_ref=source, dst_ref=full.at[si, twin], send_sem=local_sem.at[6], recv_sem=recv_sem.at[receive],
            device_id={"box": box, "sample": sample}, device_id_type=MESH,
        ).start()

    other_twin = (twin + 1) % twins
    handed = 1
    if twins > 1:
        other_box = level * twins + other_twin
        cross[...] = coarse(other_box)
        for off in range(ns - 1, -1, -1):
            hand(cross, 3, other_box, (si + off) % ns)
        handed += ns
    full[si, twin] = coarse(bi)
    hand(full.at[si, twin], 2, bi, (si + 1) % ns)

    arrive_b()
    ready("leaf_src", "leaf_op", "leaf_ops")
    incoming = []
    for b in range(boxes):
        total = None
        for j in range(leaf_src.shape[1]):
            source = pat[jnp.clip(leaf_src[b, j] - (dev - 1) * boxes, 0, 3 * boxes - 1)]
            term = translate(leaf_ops, leaf_op[b, j], source)
            total = term if total is None else total + term
        incoming.append(total)


    def lower(slot, t):
        values = full[halves[slot], t]
        lowered = jnp.concatenate(
            [
                inward(values * phases[slot, t, 0, b : b + 1, :], values * phases[slot, t, 1, b : b + 1, :])
                for b in range(boxes)
            ],
            axis=0,
        )
        return both(lowered, interp[slot, t], 1)

    lowered = lower(0, twin)
    bulk(cross, 6, 2).wait_recv()
    lowered = lowered + lower(1, twin)
    if twins > 1:
        bulk(gathered.at[pl.ds(0, ns)], 6, 3).wait_recv()
        for slot in range(ns):
            lowered = lowered + lower(slot, other_twin)
    for b in range(boxes):
        incoming[b] = incoming[b] + lowered[b * rows : (b + 1) * rows]

    lane = lax.broadcasted_iota(jnp.int32, (rows, 128), 1)
    row = lax.broadcasted_iota(jnp.int32, (rows, 128), 0)
    square = jnp.zeros((rows, 1), F32)
    straight = [jnp.zeros((rows, 1), F32) for _ in range(vectors)]
    crossed = [jnp.zeros((rows, 1), F32) for _ in range(vectors)]
    for e in range(ells):
        arriving = incoming[0] * member[0][e]
        for b in range(1, boxes):
            arriving = arriving + incoming[b] * member[b][e]
        far = inward(both(arriving, cos_tab[e], 0), both(arriving, sin_tab[e], 0))
        value = ks[vectors - 1, e] + near_acc[e] + far * leaf_width ** (-0.5)
        result[e] = value
        other = swap(value)
        square = square + jnp.sum(value * value, axis=1, keepdims=True)
        for m in range(vectors):
            basis = ks[m, e]
            straight[m] = straight[m] + jnp.sum(basis * value, axis=1, keepdims=True)
            crossed[m] = crossed[m] + jnp.sum(basis * other, axis=1, keepdims=True)
    packed = jnp.where(lane == vectors * rows + row, jnp.broadcast_to(square, lane.shape), 0.0)
    for m in range(vectors):
        a = jnp.broadcast_to(straight[m], lane.shape)
        b = jnp.broadcast_to(crossed[m], lane.shape)
        dots = jnp.where(row < inc, a + swap(a), swap(b) - b)
        packed = packed + jnp.where(lane == m * rows + row, dots, 0.0)
    sums[dev] = jnp.sum(packed, axis=0, keepdims=True)
    def share(box, sample):
        pltpu.make_async_remote_copy(
            src_ref=sums.at[dev], dst_ref=sums.at[dev], send_sem=local_sem.at[7], recv_sem=recv_sem.at[4],
            device_id={"box": box, "sample": sample}, device_id_type=MESH,
        ).start()

    for distance in range(levels - 1, 0, -1):
        for there, up in ((level + distance < levels, 1), (level >= distance, -1)):
            @pl.when(there)
            def _(distance=distance, up=up):
                for turned in range(twins):
                    for flip in range(ns):
                        share((level + up * distance) * twins + (bi + turned) % twins, (si + flip) % ns)
    for near in range(twins * ns - 1, 0, -1):
        share(level * twins + (bi + near // ns) % twins, (si + near % ns) % ns)
    every_sum = bulk(sums.at[pl.ds(0, nd - 1)], 7, 4)
    every_sum.wait_recv()
    total = sums[0]
    for index in range(1, nd):
        total = total + sums[index]
    total = total * (1.0 / (ells * nodes * nd))
    spread = jnp.broadcast_to(total, lane.shape)

    def column(start):
        return jnp.sum(
            jnp.where(lane == start + lax.rem(row, inc), spread, 0.0), axis=1, keepdims=True
        )

    real = [column(m * rows) for m in range(vectors)]
    imag = [column(m * rows + inc) for m in range(vectors)]
    norm_sq = column(vectors * rows) + column(vectors * rows + inc)
    for m in range(vectors):
        norm_sq = norm_sq - (real[m] * real[m] + imag[m] * imag[m])
    norm = jnp.sqrt(norm_sq)
    for m in range(vectors):
        for q in range(2):
            at = m * rows + q * inc
            small_out[q * vectors + m : q * vectors + m + 1, 0:inc] = total[:, at : at + inc]
    flat = jnp.sum(
        jnp.where((lane == row) & (row < inc), jnp.broadcast_to(norm, lane.shape), 0.0), axis=0, keepdims=True
    )
    small_out[2 * vectors : 2 * vectors + 1, :] = flat
    for e in range(ells):
        kept = result[e]
        for m in range(vectors):
            basis = ks[m, e]
            kept = kept - inward(basis * real[m], basis * imag[m])
        kept = kept / norm
        for q in range(2):
            next_out[q, e] = kept[q * inc : (q + 1) * inc]
    outs = [
        pltpu.make_async_copy(next_out, next_hbm, local_sem.at[8]),
        pltpu.make_async_copy(small_out, small_hbm, local_sem.at[9]),
    ]
    for copy in outs:
        copy.start()

    finish_a()
    finish_b()
    bulk(gathered.at[pl.ds(0, handed)], 6, 2).wait_send()
    swap_parts.wait_send()
    every_parent.wait_send()
    every_sum.wait_send()
    for copy in outs:
        copy.wait()


def hand_on(small_in, next_in, h_out, norm_out, next_out):
    _, vectors, inc = h_out.shape
    next_out[...] = next_in[...]
    for q in range(2):
        h_out[q] = small_in[q * vectors : (q + 1) * vectors, 0:inc]
    norm_out[...] = small_in[2 * vectors : 2 * vectors + 1, 0:inc]


def body(
    nb,
    ns,
    krylov,
    self_inv,
    node_pos,
    node_wts,
    box_of,
    near_list,
    leaf_src,
    leaf_op,
    leaf_ops,
    interp,
    parent_centers,
    up_src,
    up_op,
    up_ops,
):
    _, vectors, inc, ells, nodes = krylov.shape
    rows = 2 * inc
    boxes = leaf_src.shape[0]
    leaf_width, up_width = interp.shape
    half = up_ops.shape[2]
    nd = nb * ns
    twins = 2 if nb % 2 == 0 else 1
    part = half // twins
    directions = sphere_points(leaf_width).T
    pieces = []
    for _ in range(3):
        pieces.append(directions.astype(BF16))
        directions = directions - pieces[-1].astype(np.float32)
    leaf_dirs = np.zeros((leaf_width, 8 * len(SPLITS)), BF16)
    for block, (piece, _) in enumerate(SPLITS):
        leaf_dirs[:, 8 * block : 8 * block + 3] = pieces[piece]
    up_dirs = np.zeros((ns, 8, half), np.float32)
    up_dirs[:, :3] = np.moveaxis(sphere_points(up_width).reshape(3, ns, half), 1, 0)
    small = [box_of, near_list, leaf_src, leaf_op, up_src, up_op, parent_centers.T]
    large = [jnp.transpose(krylov, (0, 1, 3, 2, 4)), self_inv, node_pos, node_wts]
    large += [jnp.asarray(leaf_dirs), jnp.asarray(up_dirs)]
    vmem = pl.BlockSpec(memory_space=pltpu.VMEM)
    hbm = pl.BlockSpec(memory_space=pl.ANY)
    dma = pltpu.SemaphoreType.DMA
    shapes = (
        jax.ShapeDtypeStruct((2, vectors, inc), F32),
        jax.ShapeDtypeStruct((1, inc), F32),
        jax.ShapeDtypeStruct((2, ells, inc, nodes), F32),
    )
    small_shape = jax.ShapeDtypeStruct((16 * ((2 * vectors + 16) // 16), 128), F32)
    small_rows, next_rows = pl.pallas_call(
        functools.partial(kernel, nb, ns),
        out_shape=(small_shape, shapes[2]),
        in_specs=[hbm] * 16,
        out_specs=(hbm, hbm),
        scratch_shapes=[pltpu.SMEM(x.shape, x.dtype) for x in small]
        + [pltpu.VMEM(x.shape, x.dtype) for x in large]
        + [
            pltpu.VMEM(leaf_ops.shape, F32),
            pltpu.VMEM((ns, leaf_width, half), F32),
            pltpu.VMEM((*up_ops.shape[:2], part), F32),
            pltpu.VMEM((ns, twins, leaf_width, part), BF16),
            pltpu.VMEM((vectors, ells, rows, nodes), F32),
            pltpu.VMEM((3 * ells, rows + 8, nodes), F32),
            pltpu.VMEM((ns, twins, 2, boxes, part), F32),
            pltpu.VMEM((ells, nodes, 8 * len(SPLITS) + 16), BF16),
            pltpu.VMEM((ells, 8 * len(SPLITS), nodes), BF16),
            pltpu.VMEM((ells, leaf_width, nodes), F32),
            pltpu.VMEM((ells, leaf_width, nodes), BF16),
            pltpu.VMEM((ells, leaf_width, nodes), BF16),
            pltpu.VMEM((3 * boxes, rows, leaf_width), F32),
            pltpu.VMEM((twins, rows, part), F32),
            pltpu.VMEM((twins, rows, part), F32),
            pltpu.VMEM((twins, rows, part), F32),
            pltpu.VMEM((nb, rows, part), F32),
            pltpu.VMEM((rows, part), F32),
            pltpu.VMEM((ns, twins, rows, part), F32),
            pltpu.VMEM((2, nodes, nodes), F32),
            pltpu.VMEM((2, nodes, nodes), BF16),
            pltpu.VMEM((2, nodes, nodes), BF16),
            pltpu.VMEM((ells, rows, nodes), F32),
            pltpu.VMEM((ells, rows, nodes), F32),
            pltpu.VMEM((nd, 1, 128), F32),
            dma((ns + 15,)),
            dma((2,)),
            dma((2,)),
            dma((5,)),
            pltpu.VMEM(small_shape.shape, F32),
            pltpu.VMEM(shapes[2].shape, F32),
        ],
        compiler_params=pltpu.CompilerParams(
            collective_id=0, has_side_effects=True, vmem_limit_bytes=67043328
        ),
    )(*small, *large, leaf_ops, interp, up_ops)
    h_column, h_norm, next_vector = pl.pallas_call(
        hand_on,
        out_shape=shapes,
        in_specs=[vmem] * 2,
        out_specs=(vmem, vmem, vmem),
    )(small_rows, next_rows)
    return h_column, h_norm.reshape(inc), jnp.transpose(next_vector, (0, 2, 1, 3))


def solution(mesh):
    placed = (
        P(None, None, None, ("group", "box", "sample"), None),
        P(None, ("group", "box", "sample"), None, None),
        P(None, ("group", "box", "sample"), None),
        P(("group", "box", "sample"), None),
        P(("group", "box", "sample")),
        P(("group", "box", "sample"), None),
        P(("group", "box", "sample"), None),
        P(("group", "box", "sample"), None),
        P(),
        P(),
        P(None, ("group", "box")),
        P("group", None),
        P("group", None),
        P(None, None, "sample"),
    )
    return jax.shard_map(
        functools.partial(body, mesh.shape["box"], mesh.shape["sample"]),
        mesh=mesh,
        in_specs=placed,
        out_specs=(P(None, None, "group"), P("group"), P(None, None, ("box", "sample"), "group")),
        check_vma=False,
    )
```

```python
import functools
import math

import jax
import jax.numpy as jnp
import numpy as np
from jax import lax
from jax.experimental import pallas as pl
from jax.experimental.pallas import tpu as pltpu
from jax.sharding import PartitionSpec as P

MESH = pl.DeviceIdType.MESH
F32 = jnp.float32
BF16 = jnp.bfloat16
ROWS = 64
SPAN = 128
TEAM = 4
LATE = 8
SPLITS = ((0, 0), (1, 0), (2, 0), (0, 1), (1, 1), (0, 2))


def sphere_points(total):
    position = np.arange(total).astype(np.float32)
    height = np.float32(1.0) - (np.float32(2.0) * position + np.float32(1.0)) / np.float32(total)
    radius = np.sqrt(np.float32(1.0) - height * height)
    angle = (position * np.float32(math.pi * (3.0 - math.sqrt(5.0)))).astype(np.float64)
    points = [radius * np.cos(angle).astype(np.float32), radius * np.sin(angle).astype(np.float32), height]
    return np.stack(points).astype(np.float32)


SIN_TABLE = (4.44286798223381, -7.307445412162602, 3.594802094687321, -0.7844036018968589)
COS_TABLE = (1.414204080580398, -6.977642059296966, 5.715238406047747, -1.7283486673722932)
SIN_FULL = (4.442882834891658, -7.308241184631927, 3.6062893308970487, -0.8457654001243101, 0.10920874958601288)
COS_FULL = (1.4142134965660362, -6.978850988281385, 5.739461171112273, -1.88356298861798, 0.31069819238699753)


def series(coefs, u):
    total = coefs[-1]
    for coef in coefs[-2::-1]:
        total = total * u + coef
    return total


def half_turn(t, sin_coefs, cos_coefs):
    f = t - jnp.round(t)
    u = f * f
    return series(sin_coefs, u) * f, series(cos_coefs, u)


def turn(t, sin_coefs=SIN_TABLE, cos_coefs=COS_TABLE):
    s, c = half_turn(t, sin_coefs, cos_coefs)
    return 1.0 - s * s, s * c


def thirds(x):
    high = x.astype(BF16).astype(F32)
    rest = x - high
    middle = rest.astype(BF16).astype(F32)
    return high, middle, rest - middle


def pair(x):
    high = x.astype(BF16).astype(F32)
    return jnp.concatenate([high, x - high], axis=0).astype(BF16)


def both(x, table, contract):
    rows = x.shape[0]
    out = lax.dot_general(
        pair(x), table, (((1,), (contract,)), ((), ())), preferred_element_type=F32
    )
    return out[:rows] + out[rows:]


def kernel(
    box_count_axis,
    sample_count_axis,
    box_of_hbm,
    near_list_hbm,
    leaf_src_hbm,
    leaf_op_hbm,
    up_src_hbm,
    up_op_hbm,
    parent_centers_hbm,
    krylov_hbm,
    self_inv_hbm,
    node_pos_hbm,
    node_wts_hbm,
    leaf_dirs_hbm,
    up_dirs_hbm,
    leaf_ops_hbm,
    interp_hbm,
    up_ops_hbm,
    sums_hbm,
    result_hbm,
    box_of,
    near_list,
    leaf_src,
    leaf_op,
    up_src,
    up_op,
    parent_centers,
    krylov,
    self_inv,
    node_pos,
    node_wts,
    leaf_dirs,
    up_dirs,
    leaf_ops,
    interp_raw,
    up_ops,
    interp,
    ks,
    halo,
    phases,
    columns,
    split_pos,
    turns,
    cos_tab,
    sin_tab,
    pat,
    give,
    take,
    parents,
    gathered,
    cross,
    full,
    squares,
    near_r,
    near_i,
    near_acc,
    result,
    share_row,
    local_sem,
    recv_a,
    recv_b,
    recv_sem,
):
    nb, ns = box_count_axis, sample_count_axis
    nd = nb * ns
    _, vectors, ells, inc, nodes = krylov.shape
    rows = 2 * inc
    boxes = leaf_src.shape[0]
    near_count = near_list.shape[1]
    team, leaf_width, part = interp.shape[1:]
    half = team * part
    pairs_total = ells * near_count
    bi = lax.axis_index("box")
    si = lax.axis_index("sample")
    dev = bi * ns + si
    twins = 2 if nb % 2 == 0 else 1
    levels = nb // twins
    level = bi // twins
    member_of_team = bi % team
    groups = nb // team

    def wrapped(value, size):
        return jnp.where(value >= size, value - size, value)

    own_group = bi // team
    bases = [wrapped(own_group + 1 + g, groups) * team for g in range(groups - 1)] + [own_group * team]
    cores = [si] + [wrapped(si + flip, ns) for flip in range(1, ns)]

    def load(slot, source, target):
        copy = pltpu.make_async_copy(source, target, local_sem.at[slot])
        copy.start()
        return copy

    loads = {}

    def begin(**arrays):
        for name, (source, target) in arrays.items():
            loads[name] = load(len(loads), source, target)

    def ready(*wanted):
        for name in wanted:
            loads[name].wait()

    def place(index):
        return {"box": index // ns, "sample": index % ns}

    begin(box_of=(box_of_hbm, box_of), node_pos=(node_pos_hbm, node_pos), leaf_dirs=(leaf_dirs_hbm, leaf_dirs))
    barrier = pltpu.get_barrier_semaphore()
    def all_others(act):
        for base in bases[:-1]:
            for t in range(team):
                for core in cores:
                    act(base + t, core)
        for turn_by in range(team):
            for core in cores[1 if turn_by == 0 else 0 :]:
                act(bases[-1] + wrapped(member_of_team + turn_by, team), core)

    all_others(
        lambda box, core: pl.semaphore_signal(
            barrier, inc=1, device_id={"box": box, "sample": core}, device_id_type=MESH
        )
    )
    begin(
        krylov=(krylov_hbm, krylov), node_wts=(node_wts_hbm, node_wts), self_inv=(self_inv_hbm, self_inv),
        parent_centers=(parent_centers_hbm, parent_centers), up_dirs=(up_dirs_hbm, up_dirs),
    )
    halves = cores[:2]

    def begin_interp(slot):
        at = pl.ds(pl.multiple_of(halves[slot] * half, half), half)
        loads["interp", slot] = load(len(loads), interp_hbm.at[:, at], interp_raw.at[slot])

    begin_interp(1)

    sign = jnp.where(lax.broadcasted_iota(jnp.int32, (rows, 1), 0) < inc, 1.0, -1.0)

    def swap(x):
        return pltpu.roll(x, inc, 0)

    def inward(c, d):
        return c - sign * swap(d)

    def outward(c, d):
        return c + sign * swap(d)

    def neighbours(buffer, width, send, recv):
        own = buffer.at[pl.ds(width, width)]
        right = pltpu.make_async_remote_copy(
            src_ref=own, dst_ref=buffer.at[pl.ds(0, width)], send_sem=local_sem.at[send], recv_sem=recv.at[0],
            device_id=place((dev + 1) % nd), device_id_type=MESH,
        )
        left = pltpu.make_async_remote_copy(
            src_ref=own, dst_ref=buffer.at[pl.ds(2 * width, width)], send_sem=local_sem.at[send + 1], recv_sem=recv.at[1],
            device_id=place((dev + nd - 1) % nd), device_id_type=MESH,
        )

        def start():
            @pl.when(dev < nd - 1)
            def _():
                right.start()

            @pl.when(dev > 0)
            def _():
                left.start()

        def arrive():
            @pl.when(dev > 0)
            def _():
                right.wait_recv()

            @pl.when(dev < nd - 1)
            def _():
                left.wait_recv()

        def finish():
            @pl.when(dev < nd - 1)
            def _():
                right.wait_send()

            @pl.when(dev > 0)
            def _():
                left.wait_send()

        return start, arrive, finish

    start_a, arrive_a, finish_a = neighbours(halo, ells, 0, recv_a)
    start_b, arrive_b, finish_b = neighbours(pat, boxes, 2, recv_b)

    ready("node_pos", "box_of")
    for e in range(ells):
        for axis in range(3):
            halo[ells + e, rows + axis : rows + axis + 1, :] = node_pos[axis, e : e + 1, :]
        halo[ells + e, rows + 3 :, :] = jnp.zeros((halo.shape[1] - rows - 3, nodes), F32)

    member = [
        [jnp.where(box_of[e] - dev * boxes == b, 1.0, 0.0) for e in range(ells)] for b in range(boxes)
    ]
    position_sum = [
        jnp.sum(halo[ells + e, rows : rows + 8, :], axis=1, keepdims=True) for e in range(ells)
    ]
    centers = []
    for b in range(boxes):
        total = position_sum[0] * member[b][0]
        amount = member[b][0]
        for e in range(1, ells):
            total = total + position_sum[e] * member[b][e]
            amount = amount + member[b][e]
        centers.append(total / (jnp.full((8, 1), 1.0, F32) * (amount * nodes)))
    for e in range(ells):
        middle = centers[0] * member[0][e]
        for b in range(1, boxes):
            middle = middle + centers[b] * member[b][e]
        here = halo[ells + e, rows : rows + 8, :]
        pieces = thirds(here - middle)
        split_pos[e] = jnp.concatenate([pieces[p] for _, p in SPLITS], axis=0).astype(BF16)

    nt = (((1,), (1,)), ((), ()))
    spans = [pl.ds(start, SPAN) for start in range(0, leaf_width, SPAN)]

    def angles(e, span):
        turns[e, span, :] = jnp.dot(leaf_dirs[span, :], split_pos[e], preferred_element_type=F32)

    def fill(e, span):
        cosine, sine = turn(turns[e, span, :])
        cos_tab[e, span, :] = cosine.astype(BF16)
        sin_tab[e, span, :] = sine.astype(BF16)

    def gather_up(e, span):
        c = lax.dot_general(pairs[e], cos_tab[e, span, :], nt, preferred_element_type=F32)
        d = lax.dot_general(pairs[e], sin_tab[e, span, :], nt, preferred_element_type=F32)
        piece = outward(c[:rows] + c[rows:], d[:rows] + d[rows:])
        for b in range(boxes):
            part = piece * member[b][e]
            pat[boxes + b, :, span] = part if e == 0 else pat[boxes + b, :, span] + part

    ready("leaf_dirs")
    for span in spans:
        angles(0, span)
    for span in spans:
        if ells > 1:
            angles(1, span)
        fill(0, span)

    ready("krylov", "node_wts", "self_inv", "parent_centers", "up_dirs")
    begin_interp(0)
    begin(
        near_list=(near_list_hbm, near_list), leaf_src=(leaf_src_hbm, leaf_src), leaf_op=(leaf_op_hbm, leaf_op),
        up_src=(up_src_hbm, up_src), up_op=(up_op_hbm, up_op),
        up_ops=(up_ops_hbm.at[:, :, pl.ds(pl.multiple_of(member_of_team * part, part), part)], up_ops),
        leaf_ops=(leaf_ops_hbm, leaf_ops),
    )
    pairs = []
    for e in range(ells):
        rounded = jnp.concatenate([krylov[q, vectors - 1, e] for q in range(2)], axis=0).astype(BF16)
        c = lax.dot_general(rounded, self_inv[0, e], nt, preferred_element_type=F32)
        d = lax.dot_general(rounded, self_inv[1, e], nt, preferred_element_type=F32)
        source = inward(c, d) * node_wts[e : e + 1, :]
        halo[ells + e, 0:rows, :] = source
        pairs.append(pair(source))


    def up_phase(center, dirs):
        t = (center[0:1] - parent_centers[0, 0]) * dirs[0:1]
        for axis in range(1, 3):
            t = t + (center[axis : axis + 1] - parent_centers[0, axis]) * dirs[axis : axis + 1]
        return t

    def turns_of(list_of_centers, dirs):
        t = jnp.concatenate([up_phase(center, dirs) for center in list_of_centers], axis=0)
        return turn(t, SIN_FULL, COS_FULL)

    for slot, h in enumerate(halves):
        cosine, sine = turns_of(centers, up_dirs[h])
        for t in range(team):
            phases[slot, t, 0] = cosine[:, t * part : (t + 1) * part]
            phases[slot, t, 1] = sine[:, t * part : (t + 1) * part]

    pending = [(0, span) for span in spans] if ells > 1 else []
    for e in range(min(1, ells - 1), ells):
        for span in spans:
            if e + 1 < ells:
                angles(e + 1, span)
            if e > 0:
                fill(e, span)
            for _ in range(min(len(pending), 2 if e > 1 else 1)):
                gather_up(*pending.pop(0))
            pending.append((e, span))
    for item in pending:
        gather_up(*item)

    whole = pair(jnp.concatenate([pat[boxes + b] for b in range(boxes)], axis=0))

    def lift(slot, t):
        table = interp_raw[slot, :, t * part : (t + 1) * part].astype(BF16)
        interp[slot, t] = table
        lifted = jnp.dot(whole, table, preferred_element_type=F32)
        lifted = lifted[: boxes * rows] + lifted[boxes * rows :]
        parent = None
        for b in range(boxes):
            piece = lifted[b * rows : (b + 1) * rows]
            term = outward(
                piece * phases[slot, t, 0, b : b + 1, :], piece * phases[slot, t, 1, b : b + 1, :]
            )
            parent = term if parent is None else parent + term
        return parent

    partner_id = {"box": bi, "sample": cores[1]}

    def swap_part(t):
        return pltpu.make_async_remote_copy(
            src_ref=give.at[t], dst_ref=take.at[t], send_sem=local_sem.at[4], recv_sem=recv_sem.at[6 + t],
            device_id=partner_id, device_id_type=MESH,
        )

    def bulk(ref, send, receive):
        return pltpu.make_async_remote_copy(
            src_ref=ref, dst_ref=ref, send_sem=local_sem.at[send], recv_sem=recv_sem.at[receive],
            device_id=partner_id, device_id_type=MESH,
        )

    def deliver(box, t):
        pltpu.make_async_remote_copy(
            src_ref=parents.at[t], dst_ref=gathered.at[bi], send_sem=local_sem.at[5],
            recv_sem=recv_sem.at[1], device_id={"box": box, "sample": si}, device_id_type=MESH,
        ).start()

    ready(("interp", 1))
    for t in range(team):
        give[t] = lift(1, t)
    pl.semaphore_wait(barrier, nd - 1)
    for t in range(team):
        swap_part(t).start()
    start_a()
    ready(("interp", 0))
    own_part = [lift(0, t) for t in range(team)]
    for t in range(team):
        swap_part(t).wait_recv()
        parents[t] = own_part[t] + take[t]
        for base in bases[:-1]:
            deliver(base + t, t)

        @pl.when(member_of_team != t)
        def _(t=t):
            deliver(bases[-1] + t, t)

    every_parent = bulk(gathered.at[pl.ds(0, nb - 1)], 5, 1)
    gathered[bi] = parents[member_of_team]
    start_b()

    def edge(x, first, ones):
        parts = thirds(jnp.sum(x * x, axis=0, keepdims=True))
        at = lax.broadcasted_iota(jnp.int32, x.shape, 0)
        block = jnp.where((at >= ones) & (at < ones + 3), 1.0, 0.0)
        for p in range(3):
            block = jnp.where(at == first + p, jnp.broadcast_to(parts[p], x.shape), block)
        return block

    for e in range(ells):
        x = halo[ells + e, rows : rows + 8, :] - position_sum[e] * (1.0 / nodes)
        pieces = thirds(-2.0 * x)
        blocks = [pieces[p] for p, _ in SPLITS] + [edge(x, 3, 0)]
        blocks.append(jnp.zeros_like(x))
        columns[e] = jnp.transpose(jnp.concatenate(blocks, axis=0)).astype(BF16)
        for m in range(vectors):
            for q in range(2):
                ks[m, e, q * inc : (q + 1) * inc, :] = krylov[q, m, e]

    def translate(operators, index, values):
        pair_rows = operators[index]
        return inward(values * pair_rows[0:1], values * pair_rows[1:2])

    ready("near_list")
    arrive_a()
    near_acc[...] = jnp.zeros(near_acc.shape, F32)

    near_items = [(e, j) for e in range(ells) for j in range(near_count)]

    def near_source(e, j):
        return halo[jnp.clip(near_list[e, j] - (dev - 1) * ells, 0, 3 * ells - 1)]

    def distances(index):
        e, j = near_items[index]
        y = near_source(e, j)[rows : rows + 8] - position_sum[e] * (1.0 / nodes)
        pieces = thirds(y)
        blocks = [pieces[p] for _, p in SPLITS] + [edge(y, 0, 3), jnp.zeros_like(y)]
        split = jnp.concatenate(blocks, axis=0).astype(BF16)
        for chunk in range(0, nodes, ROWS):
            squares[index % 2, chunk : chunk + ROWS, :] = jnp.dot(
                columns[e, chunk : chunk + ROWS, :], split, preferred_element_type=F32
            )

    def near_pair(index):
        e, j = near_items[index]
        slot = index % 2
        for chunk in range(0, nodes, ROWS):
            squared = squares[slot, chunk : chunk + ROWS, :]
            inverse = lax.rsqrt(squared)
            s, c = half_turn(squared * inverse, SIN_TABLE, COS_TABLE)
            scaled = s * inverse
            near_r[slot, chunk : chunk + ROWS, :] = (inverse - s * scaled).astype(BF16)
            near_i[slot, chunk : chunk + ROWS, :] = (scaled * c).astype(BF16)
        values = near_source(e, j)[0:rows]
        near_acc[e] += inward(both(values, near_r[slot], 1), both(values, near_i[slot], 1))

    def near_run(start, stop):
        if start < stop:
            distances(start)
        for index in range(start, stop):
            if index + 1 < stop:
                distances(index + 1)
            near_pair(index)

    early = pairs_total - min(LATE, pairs_total)
    near_run(0, early)

    ready("up_src", "up_op", "up_ops")
    every_parent.wait_recv()

    def coarse(box):
        total = None
        for j in range(up_src.shape[1]):
            term = translate(up_ops, up_op[box, j], gathered[up_src[box, j]])
            total = term if total is None else total + term
        return total

    mine = si * team + member_of_team
    first_box = bi - member_of_team
    team_levels = team // twins if team > 1 else 1

    def hand(source, receive, box, sample):
        pltpu.make_async_remote_copy(
            src_ref=source, dst_ref=full.at[mine], send_sem=local_sem.at[6], recv_sem=recv_sem.at[receive],
            device_id={"box": box, "sample": sample}, device_id_type=MESH,
        ).start()

    def mate(rise, turned):
        return ((member_of_team // twins + rise) % team_levels) * twins + (member_of_team + turned) % twins

    close = [mate(0, turned) for turned in range(1, twins)] if team > 1 else []
    distant = [mate(rise, turned) for rise in range(team_levels - 1, 0, -1) for turned in range(twins)]
    for slot, (to, receive) in enumerate([(to, 5) for to in distant] + [(to, 3) for to in close]):
        cross[slot] = coarse(first_box + to)
        for off in range(ns - 1, -1, -1):
            hand(cross.at[slot], receive, first_box + to, (si + off) % ns)
    full[mine] = coarse(bi)
    hand(full.at[mine], 2, bi, (si + 1) % ns)
    handed = bulk(full.at[pl.ds(0, 1 + ns * (team - 1))], 6, 2)

    near_run(early, pairs_total)

    arrive_b()
    ready("leaf_src", "leaf_op", "leaf_ops")
    incoming = []
    for b in range(boxes):
        total = None
        for j in range(leaf_src.shape[1]):
            source = pat[jnp.clip(leaf_src[b, j] - (dev - 1) * boxes, 0, 3 * boxes - 1)]
            term = translate(leaf_ops, leaf_op[b, j], source)
            total = term if total is None else total + term
        incoming.append(total)


    def lower(slot, t):
        values = full[halves[slot] * team + t]
        lowered = jnp.concatenate(
            [
                inward(values * phases[slot, t, 0, b : b + 1, :], values * phases[slot, t, 1, b : b + 1, :])
                for b in range(boxes)
            ],
            axis=0,
        )
        return both(lowered, interp[slot, t], 1)

    lowered = lower(0, member_of_team)
    bulk(full.at[0], 6, 2).wait_recv()
    lowered = lowered + lower(1, member_of_team)
    for mates, receive in ((close, 3), (distant, 5)):
        if mates:
            bulk(full.at[pl.ds(0, ns * len(mates))], 6, receive).wait_recv()
        for t in mates:
            for slot in range(ns):
                lowered = lowered + lower(slot, t)
    for b in range(boxes):
        incoming[b] = incoming[b] + lowered[b * rows : (b + 1) * rows]

    lane = lax.broadcasted_iota(jnp.int32, (rows, 128), 1)
    row = lax.broadcasted_iota(jnp.int32, (rows, 128), 0)
    square = jnp.zeros((rows, 1), F32)
    straight = [jnp.zeros((rows, 1), F32) for _ in range(vectors)]
    crossed = [jnp.zeros((rows, 1), F32) for _ in range(vectors)]
    for e in range(ells):
        arriving = incoming[0] * member[0][e]
        for b in range(1, boxes):
            arriving = arriving + incoming[b] * member[b][e]
        far = inward(both(arriving, cos_tab[e], 0), both(arriving, sin_tab[e], 0))
        value = ks[vectors - 1, e] + near_acc[e] + far * leaf_width ** (-0.5)
        result[e] = value
        other = swap(value)
        square = square + jnp.sum(value * value, axis=1, keepdims=True)
        for m in range(vectors):
            basis = ks[m, e]
            straight[m] = straight[m] + jnp.sum(basis * value, axis=1, keepdims=True)
            crossed[m] = crossed[m] + jnp.sum(basis * other, axis=1, keepdims=True)
    packed = jnp.where(lane == vectors * rows + row, jnp.broadcast_to(square, lane.shape), 0.0)
    for m in range(vectors):
        a = jnp.broadcast_to(straight[m], lane.shape)
        b = jnp.broadcast_to(crossed[m], lane.shape)
        dots = jnp.where(row < inc, a + swap(a), swap(b) - b)
        packed = packed + jnp.where(lane == m * rows + row, dots, 0.0)
    share_row[...] = jnp.sum(packed, axis=0, keepdims=True)

    def share(box, sample):
        pltpu.make_async_remote_copy(
            src_ref=share_row, dst_ref=sums_hbm.at[dev], send_sem=local_sem.at[7], recv_sem=recv_sem.at[4],
            device_id={"box": box, "sample": sample}, device_id_type=MESH,
        ).start()

    all_others(share)
    outs = [
        pltpu.make_async_copy(share_row, sums_hbm.at[dev], local_sem.at[8]),
        pltpu.make_async_copy(result, result_hbm, local_sem.at[9]),
    ]
    for copy in outs:
        copy.start()
    finish_a()
    finish_b()
    handed.wait_send()
    bulk(full.at[pl.ds(0, team)], 4, 0).wait_send()
    every_parent.wait_send()
    every_sum = bulk(sums_hbm.at[pl.ds(0, nd - 1)], 7, 4)
    every_sum.wait_send()
    for copy in outs:
        copy.wait()
    every_sum.wait_recv()


def finish(sums, result, krylov, h_out, norm_out, next_out):
    _, vectors, ells, inc, nodes = krylov.shape
    rows = 2 * inc
    lane = lax.broadcasted_iota(jnp.int32, (rows, 128), 1)
    row = lax.broadcasted_iota(jnp.int32, (rows, 128), 0)
    sign = jnp.where(lax.broadcasted_iota(jnp.int32, (rows, 1), 0) < inc, 1.0, -1.0)
    total = sums[0]
    for index in range(1, sums.shape[0]):
        total = total + sums[index]
    total = total * (1.0 / (ells * nodes * sums.shape[0]))
    spread = jnp.broadcast_to(total, lane.shape)

    def column(start):
        return jnp.sum(
            jnp.where(lane == start + lax.rem(row, inc), spread, 0.0), axis=1, keepdims=True
        )

    real = [column(m * rows) for m in range(vectors)]
    imag = [column(m * rows + inc) for m in range(vectors)]
    norm_sq = column(vectors * rows) + column(vectors * rows + inc)
    for m in range(vectors):
        norm_sq = norm_sq - (real[m] * real[m] + imag[m] * imag[m])
    norm = jnp.sqrt(norm_sq)
    for m in range(vectors):
        for q in range(2):
            at = m * rows + q * inc
            h_out[q, m : m + 1, :] = total[:, at : at + inc]
    flat = jnp.sum(
        jnp.where((lane == row) & (row < inc), jnp.broadcast_to(norm, lane.shape), 0.0), axis=0, keepdims=True
    )
    norm_out[...] = flat[:, 0:inc]
    for e in range(ells):
        kept = result[e]
        for m in range(vectors):
            basis = jnp.concatenate([krylov[q, m, e] for q in range(2)], axis=0)
            kept = kept - (basis * real[m] - sign * pltpu.roll(basis * imag[m], inc, 0))
        kept = kept / norm
        for q in range(2):
            next_out[q, e] = kept[q * inc : (q + 1) * inc]


def body(
    nb,
    ns,
    krylov,
    self_inv,
    node_pos,
    node_wts,
    box_of,
    near_list,
    leaf_src,
    leaf_op,
    leaf_ops,
    interp,
    parent_centers,
    up_src,
    up_op,
    up_ops,
):
    _, vectors, inc, ells, nodes = krylov.shape
    rows = 2 * inc
    boxes = leaf_src.shape[0]
    leaf_width, up_width = interp.shape
    half = up_ops.shape[2]
    nd = nb * ns
    team = next(size for size in (TEAM, 2, 1) if nb % size == 0)
    part = half // team
    directions = sphere_points(leaf_width).T
    pieces = []
    for _ in range(3):
        pieces.append(directions.astype(BF16))
        directions = directions - pieces[-1].astype(np.float32)
    leaf_dirs = np.zeros((leaf_width, 8 * len(SPLITS)), BF16)
    for block, (piece, _) in enumerate(SPLITS):
        leaf_dirs[:, 8 * block : 8 * block + 3] = pieces[piece]
    up_dirs = np.zeros((ns, 8, half), np.float32)
    up_dirs[:, :3] = np.moveaxis(sphere_points(up_width).reshape(3, ns, half), 1, 0)
    small = [box_of, near_list, leaf_src, leaf_op, up_src, up_op, parent_centers.T]
    large = [jnp.transpose(krylov, (0, 1, 3, 2, 4)), self_inv, node_pos, node_wts]
    large += [jnp.asarray(leaf_dirs), jnp.asarray(up_dirs)]
    vmem = pl.BlockSpec(memory_space=pltpu.VMEM)
    hbm = pl.BlockSpec(memory_space=pl.ANY)
    dma = pltpu.SemaphoreType.DMA
    shapes = (
        jax.ShapeDtypeStruct((2, vectors, inc), F32),
        jax.ShapeDtypeStruct((1, inc), F32),
        jax.ShapeDtypeStruct((2, ells, inc, nodes), F32),
    )
    sums, result = pl.pallas_call(
        functools.partial(kernel, nb, ns),
        out_shape=(
            jax.ShapeDtypeStruct((nd, 1, 128), F32),
            jax.ShapeDtypeStruct((ells, rows, nodes), F32),
        ),
        in_specs=[hbm] * 16,
        out_specs=(hbm, hbm),
        scratch_shapes=[pltpu.SMEM(x.shape, x.dtype) for x in small]
        + [pltpu.VMEM(x.shape, x.dtype) for x in large]
        + [
            pltpu.VMEM(leaf_ops.shape, F32),
            pltpu.VMEM((ns, leaf_width, half), F32),
            pltpu.VMEM((*up_ops.shape[:2], part), F32),
            pltpu.VMEM((ns, team, leaf_width, part), BF16),
            pltpu.VMEM((vectors, ells, rows, nodes), F32),
            pltpu.VMEM((3 * ells, rows + 8, nodes), F32),
            pltpu.VMEM((ns, team, 2, boxes, part), F32),
            pltpu.VMEM((ells, nodes, 8 * len(SPLITS) + 16), BF16),
            pltpu.VMEM((ells, 8 * len(SPLITS), nodes), BF16),
            pltpu.VMEM((ells, leaf_width, nodes), F32),
            pltpu.VMEM((ells, leaf_width, nodes), BF16),
            pltpu.VMEM((ells, leaf_width, nodes), BF16),
            pltpu.VMEM((3 * boxes, rows, leaf_width), F32),
            pltpu.VMEM((team, rows, part), F32),
            pltpu.VMEM((team, rows, part), F32),
            pltpu.VMEM((team, rows, part), F32),
            pltpu.VMEM((nb, rows, part), F32),
            pltpu.VMEM((team, rows, part), F32),
            pltpu.VMEM((ns * team, rows, part), F32),
            pltpu.VMEM((2, nodes, nodes), F32),
            pltpu.VMEM((2, nodes, nodes), BF16),
            pltpu.VMEM((2, nodes, nodes), BF16),
            pltpu.VMEM((ells, rows, nodes), F32),
            pltpu.VMEM((ells, rows, nodes), F32),
            pltpu.VMEM((1, 128), F32),
            dma((ns + 15,)),
            dma((2,)),
            dma((2,)),
            dma((6 + team,)),
        ],
        compiler_params=pltpu.CompilerParams(
            collective_id=0, has_side_effects=True, vmem_limit_bytes=67043328
        ),
    )(*small, *large, leaf_ops, interp, up_ops)
    h_column, h_norm, next_vector = pl.pallas_call(
        finish,
        out_shape=shapes,
        in_specs=[vmem] * 3,
        out_specs=(vmem, vmem, vmem),
    )(sums, result, large[0])
    return h_column, h_norm.reshape(inc), jnp.transpose(next_vector, (0, 2, 1, 3))


def solution(mesh):
    placed = (
        P(None, None, None, ("group", "box", "sample"), None),
        P(None, ("group", "box", "sample"), None, None),
        P(None, ("group", "box", "sample"), None),
        P(("group", "box", "sample"), None),
        P(("group", "box", "sample")),
        P(("group", "box", "sample"), None),
        P(("group", "box", "sample"), None),
        P(("group", "box", "sample"), None),
        P(),
        P(),
        P(None, ("group", "box")),
        P("group", None),
        P("group", None),
        P(None, None, "sample"),
    )
    return jax.shard_map(
        functools.partial(body, mesh.shape["box"], mesh.shape["sample"]),
        mesh=mesh,
        in_specs=placed,
        out_specs=(P(None, None, "group"), P("group"), P(None, None, ("box", "sample"), "group")),
        check_vma=False,
    )
```

```python
import functools
import math

import jax
import jax.numpy as jnp
import numpy as np
from jax import lax
from jax.experimental import pallas as pl
from jax.experimental.pallas import tpu as pltpu
from jax.sharding import PartitionSpec as P

MESH = pl.DeviceIdType.MESH
F32 = jnp.float32
BF16 = jnp.bfloat16
ROWS = 64
SPAN = 128
TEAM = 4
LATE = 8
SPLITS = ((0, 0), (1, 0), (2, 0), (0, 1), (1, 1), (0, 2))


def sphere_points(total):
    position = np.arange(total).astype(np.float32)
    height = np.float32(1.0) - (np.float32(2.0) * position + np.float32(1.0)) / np.float32(total)
    radius = np.sqrt(np.float32(1.0) - height * height)
    angle = (position * np.float32(math.pi * (3.0 - math.sqrt(5.0)))).astype(np.float64)
    points = [radius * np.cos(angle).astype(np.float32), radius * np.sin(angle).astype(np.float32), height]
    return np.stack(points).astype(np.float32)


SIN_TABLE = (4.44286798223381, -7.307445412162602, 3.594802094687321, -0.7844036018968589)
COS_TABLE = (1.414204080580398, -6.977642059296966, 5.715238406047747, -1.7283486673722932)
SIN_FULL = (4.442882834891658, -7.308241184631927, 3.6062893308970487, -0.8457654001243101, 0.10920874958601288)
COS_FULL = (1.4142134965660362, -6.978850988281385, 5.739461171112273, -1.88356298861798, 0.31069819238699753)


def series(coefs, u):
    total = coefs[-1]
    for coef in coefs[-2::-1]:
        total = total * u + coef
    return total


def half_turn(t, sin_coefs, cos_coefs):
    f = t - jnp.round(t)
    u = f * f
    return series(sin_coefs, u) * f, series(cos_coefs, u)


def turn(t, sin_coefs=SIN_TABLE, cos_coefs=COS_TABLE):
    s, c = half_turn(t, sin_coefs, cos_coefs)
    return 1.0 - s * s, s * c


def thirds(x):
    high = x.astype(BF16).astype(F32)
    rest = x - high
    middle = rest.astype(BF16).astype(F32)
    return high, middle, rest - middle


def pair(x):
    high = x.astype(BF16).astype(F32)
    return jnp.concatenate([high, x - high], axis=0).astype(BF16)


def both(x, table, contract):
    rows = x.shape[0]
    out = lax.dot_general(
        pair(x), table, (((1,), (contract,)), ((), ())), preferred_element_type=F32
    )
    return out[:rows] + out[rows:]


def kernel(
    box_count_axis,
    sample_count_axis,
    box_of_hbm,
    near_list_hbm,
    leaf_src_hbm,
    leaf_op_hbm,
    up_src_hbm,
    up_op_hbm,
    parent_centers_hbm,
    krylov_hbm,
    self_inv_hbm,
    node_pos_hbm,
    node_wts_hbm,
    leaf_dirs_hbm,
    up_dirs_hbm,
    leaf_ops_hbm,
    interp_hbm,
    up_ops_hbm,
    sums_hbm,
    result_hbm,
    box_of,
    near_list,
    leaf_src,
    leaf_op,
    up_src,
    up_op,
    parent_centers,
    krylov,
    self_inv,
    node_pos,
    node_wts,
    leaf_dirs,
    up_dirs,
    leaf_ops,
    interp_raw,
    up_ops,
    interp,
    ks,
    halo,
    phases,
    columns,
    split_pos,
    turns,
    cos_tab,
    sin_tab,
    pat,
    give,
    take,
    parents,
    gathered,
    cross,
    full,
    squares,
    near_r,
    near_i,
    near_acc,
    result,
    share_row,
    local_sem,
    recv_a,
    recv_b,
    recv_sem,
):
    nb, ns = box_count_axis, sample_count_axis
    nd = nb * ns
    _, vectors, ells, inc, nodes = krylov.shape
    rows = 2 * inc
    boxes = leaf_src.shape[0]
    near_count = near_list.shape[1]
    team, leaf_width, part = interp.shape[1:]
    half = team * part
    pairs_total = ells * near_count
    bi = lax.axis_index("box")
    si = lax.axis_index("sample")
    dev = bi * ns + si
    twins = 2 if nb % 2 == 0 else 1
    levels = nb // twins
    level = bi // twins
    member_of_team = bi % team
    groups = nb // team

    def wrapped(value, size):
        return jnp.where(value >= size, value - size, value)

    own_group = bi // team
    bases = [wrapped(own_group + 1 + g, groups) * team for g in range(groups - 1)] + [own_group * team]
    cores = [si] + [wrapped(si + flip, ns) for flip in range(1, ns)]

    def load(slot, source, target):
        copy = pltpu.make_async_copy(source, target, local_sem.at[slot])
        copy.start()
        return copy

    loads = {}

    def begin(first, **arrays):
        for slot, (name, (source, target)) in enumerate(arrays.items()):
            loads[name] = load(first + slot, source, target)

    def ready(*wanted):
        for name in wanted:
            loads[name].wait()

    def place(index):
        return {"box": index // ns, "sample": index % ns}

    begin(0, box_of=(box_of_hbm, box_of), node_pos=(node_pos_hbm, node_pos), leaf_dirs=(leaf_dirs_hbm, leaf_dirs))
    barrier = pltpu.get_barrier_semaphore()
    shift = 0
    far_first = [wrapped(t + shift, team) for t in range(team)]

    def all_others(act):
        for base in bases[:-1]:
            for t in far_first:
                for core in cores:
                    act(base + t, core)
        for turn_by in range(team):
            for core in cores[1 if turn_by == 0 else 0 :]:
                act(bases[-1] + wrapped(member_of_team + turn_by, team), core)

    all_others(
        lambda box, core: pl.semaphore_signal(
            barrier, inc=1, device_id={"box": box, "sample": core}, device_id_type=MESH
        )
    )
    begin(
        3, krylov=(krylov_hbm, krylov), node_wts=(node_wts_hbm, node_wts), self_inv=(self_inv_hbm, self_inv),
        parent_centers=(parent_centers_hbm, parent_centers), up_dirs=(up_dirs_hbm, up_dirs),
    )
    halves = cores[:2]

    def begin_interp(slot):
        at = pl.ds(pl.multiple_of(halves[slot] * half, half), half)
        loads["interp", slot] = load(9 - slot, interp_hbm.at[:, at], interp_raw.at[slot])

    begin_interp(1)

    sign = jnp.where(lax.broadcasted_iota(jnp.int32, (rows, 1), 0) < inc, 1.0, -1.0)

    def swap(x):
        return pltpu.roll(x, inc, 0)

    def inward(c, d):
        return c - sign * swap(d)

    def outward(c, d):
        return c + sign * swap(d)

    def neighbours(buffer, width, send, recv):
        own = buffer.at[pl.ds(width, width)]
        right = pltpu.make_async_remote_copy(
            src_ref=own, dst_ref=buffer.at[pl.ds(0, width)], send_sem=local_sem.at[send], recv_sem=recv.at[0],
            device_id=place((dev + 1) % nd), device_id_type=MESH,
        )
        left = pltpu.make_async_remote_copy(
            src_ref=own, dst_ref=buffer.at[pl.ds(2 * width, width)], send_sem=local_sem.at[send + 1], recv_sem=recv.at[1],
            device_id=place((dev + nd - 1) % nd), device_id_type=MESH,
        )

        def start():
            @pl.when((si == 0) & (dev > 0))
            def _():
                left.start()

            @pl.when(dev < nd - 1)
            def _():
                right.start()

            @pl.when(si > 0)
            def _():
                left.start()

        def arrive():
            @pl.when(dev > 0)
            def _():
                right.wait_recv()

            @pl.when(dev < nd - 1)
            def _():
                left.wait_recv()

        def finish():
            @pl.when(dev < nd - 1)
            def _():
                right.wait_send()

            @pl.when(dev > 0)
            def _():
                left.wait_send()

        return start, arrive, finish

    start_a, arrive_a, finish_a = neighbours(halo, ells, 7, recv_a)
    start_b, arrive_b, finish_b = neighbours(pat, boxes, 7, recv_b)

    ready("node_pos", "box_of")
    for e in range(ells):
        for axis in range(3):
            halo[ells + e, rows + axis : rows + axis + 1, :] = node_pos[axis, e : e + 1, :]
        halo[ells + e, rows + 3 :, :] = jnp.zeros((halo.shape[1] - rows - 3, nodes), F32)

    member = [
        [jnp.where(box_of[e] - dev * boxes == b, 1.0, 0.0) for e in range(ells)] for b in range(boxes)
    ]
    position_sum = [
        jnp.sum(halo[ells + e, rows : rows + 8, :], axis=1, keepdims=True) for e in range(ells)
    ]
    centers = []
    for b in range(boxes):
        total = position_sum[0] * member[b][0]
        amount = member[b][0]
        for e in range(1, ells):
            total = total + position_sum[e] * member[b][e]
            amount = amount + member[b][e]
        centers.append(total / (jnp.full((8, 1), 1.0, F32) * (amount * nodes)))
    for e in range(ells):
        middle = centers[0] * member[0][e]
        for b in range(1, boxes):
            middle = middle + centers[b] * member[b][e]
        here = halo[ells + e, rows : rows + 8, :]
        pieces = thirds(here - middle)
        split_pos[e] = jnp.concatenate([pieces[p] for _, p in SPLITS], axis=0).astype(BF16)

    nt = (((1,), (1,)), ((), ()))
    spans = [pl.ds(start, SPAN) for start in range(0, leaf_width, SPAN)]

    def angles(e, span):
        turns[e, span, :] = jnp.dot(leaf_dirs[span, :], split_pos[e], preferred_element_type=F32)

    def fill(e, span):
        cosine, sine = turn(turns[e, span, :])
        cos_tab[e, span, :] = cosine.astype(BF16)
        sin_tab[e, span, :] = sine.astype(BF16)

    def gather_up(e, span):
        c = lax.dot_general(pairs[e], cos_tab[e, span, :], nt, preferred_element_type=F32)
        d = lax.dot_general(pairs[e], sin_tab[e, span, :], nt, preferred_element_type=F32)
        piece = outward(c[:rows] + c[rows:], d[:rows] + d[rows:])
        for b in range(boxes):
            part = piece * member[b][e]
            pat[boxes + b, :, span] = part if e == 0 else pat[boxes + b, :, span] + part

    ready("leaf_dirs")
    for span in spans:
        angles(0, span)
    for span in spans:
        if ells > 1:
            angles(1, span)
        fill(0, span)

    ready("krylov", "node_wts", "self_inv", "parent_centers", "up_dirs")
    begin_interp(0)
    begin(
        0, near_list=(near_list_hbm, near_list), leaf_src=(leaf_src_hbm, leaf_src), leaf_op=(leaf_op_hbm, leaf_op),
        up_src=(up_src_hbm, up_src), up_op=(up_op_hbm, up_op),
        up_ops=(up_ops_hbm.at[:, :, pl.ds(pl.multiple_of(member_of_team * part, part), part)], up_ops),
        leaf_ops=(leaf_ops_hbm, leaf_ops),
    )
    pairs = []
    for e in range(ells):
        rounded = jnp.concatenate([krylov[q, vectors - 1, e] for q in range(2)], axis=0).astype(BF16)
        c = lax.dot_general(rounded, self_inv[0, e], nt, preferred_element_type=F32)
        d = lax.dot_general(rounded, self_inv[1, e], nt, preferred_element_type=F32)
        source = inward(c, d) * node_wts[e : e + 1, :]
        halo[ells + e, 0:rows, :] = source
        pairs.append(pair(source))


    def up_phase(center, dirs):
        t = (center[0:1] - parent_centers[0, 0]) * dirs[0:1]
        for axis in range(1, 3):
            t = t + (center[axis : axis + 1] - parent_centers[0, axis]) * dirs[axis : axis + 1]
        return t

    def turns_of(list_of_centers, dirs):
        t = jnp.concatenate([up_phase(center, dirs) for center in list_of_centers], axis=0)
        return turn(t, SIN_FULL, COS_FULL)

    for slot, h in enumerate(halves):
        cosine, sine = turns_of(centers, up_dirs[h])
        for t in range(team):
            phases[slot, t, 0] = cosine[:, t * part : (t + 1) * part]
            phases[slot, t, 1] = sine[:, t * part : (t + 1) * part]

    pending = [(0, span) for span in spans] if ells > 1 else []
    for e in range(min(1, ells - 1), ells):
        for span in spans:
            if e + 1 < ells:
                angles(e + 1, span)
            if e > 0:
                fill(e, span)
            for _ in range(min(len(pending), 2 if e > 1 else 1)):
                gather_up(*pending.pop(0))
            pending.append((e, span))
    for item in pending:
        gather_up(*item)

    whole = pair(jnp.concatenate([pat[boxes + b] for b in range(boxes)], axis=0))

    def lift(slot, t):
        table = interp_raw[slot, :, t * part : (t + 1) * part].astype(BF16)
        interp[slot, t] = table
        lifted = jnp.dot(whole, table, preferred_element_type=F32)
        lifted = lifted[: boxes * rows] + lifted[boxes * rows :]
        parent = None
        for b in range(boxes):
            piece = lifted[b * rows : (b + 1) * rows]
            term = outward(
                piece * phases[slot, t, 0, b : b + 1, :], piece * phases[slot, t, 1, b : b + 1, :]
            )
            parent = term if parent is None else parent + term
        return parent

    partner_id = {"box": bi, "sample": cores[1]}

    def swap_part(t):
        return pltpu.make_async_remote_copy(
            src_ref=give.at[t], dst_ref=take.at[t], send_sem=local_sem.at[10], recv_sem=recv_sem.at[0],
            device_id=partner_id, device_id_type=MESH,
        )

    def bulk(ref, send, receive):
        return pltpu.make_async_remote_copy(
            src_ref=ref, dst_ref=ref, send_sem=local_sem.at[send], recv_sem=recv_sem.at[receive],
            device_id=partner_id, device_id_type=MESH,
        )

    def deliver(box, t):
        pltpu.make_async_remote_copy(
            src_ref=parents.at[t], dst_ref=gathered.at[bi], send_sem=local_sem.at[9],
            recv_sem=recv_sem.at[1], device_id={"box": box, "sample": si}, device_id_type=MESH,
        ).start()

    ready(("interp", 1))
    for t in range(team):
        give[t] = lift(1, t)
    pl.semaphore_wait(barrier, nd - 1)
    for t in range(team):
        swap_part(t).start()
    start_a()
    ready(("interp", 0))
    own_part = [lift(0, t) for t in range(team)]
    swapped = bulk(full.at[pl.ds(0, team)], 10, 0)
    swapped.wait_recv()
    for t in range(team):
        parents[t] = own_part[t] + take[t]
    for t in range(team):
        for base in bases[:-1]:
            deliver(base + t, t)

        @pl.when(member_of_team != t)
        def _(t=t):
            deliver(bases[-1] + t, t)

    every_parent = bulk(gathered.at[pl.ds(0, nb - 1)], 9, 1)
    gathered[bi] = parents[member_of_team]
    swapped.wait_send()
    finish_a()
    start_b()

    def edge(x, first, ones):
        parts = thirds(jnp.sum(x * x, axis=0, keepdims=True))
        at = lax.broadcasted_iota(jnp.int32, x.shape, 0)
        block = jnp.where((at >= ones) & (at < ones + 3), 1.0, 0.0)
        for p in range(3):
            block = jnp.where(at == first + p, jnp.broadcast_to(parts[p], x.shape), block)
        return block

    for e in range(ells):
        x = halo[ells + e, rows : rows + 8, :] - position_sum[e] * (1.0 / nodes)
        pieces = thirds(-2.0 * x)
        blocks = [pieces[p] for p, _ in SPLITS] + [edge(x, 3, 0)]
        blocks.append(jnp.zeros_like(x))
        columns[e] = jnp.transpose(jnp.concatenate(blocks, axis=0)).astype(BF16)
        for m in range(vectors):
            for q in range(2):
                ks[m, e, q * inc : (q + 1) * inc, :] = krylov[q, m, e]

    def translate(operators, index, values):
        pair_rows = operators[index]
        return inward(values * pair_rows[0:1], values * pair_rows[1:2])

    ready("near_list")
    arrive_a()
    near_acc[...] = jnp.zeros(near_acc.shape, F32)

    near_items = [(e, j) for e in range(ells) for j in range(near_count)]

    def near_source(e, j):
        return halo[jnp.clip(near_list[e, j] - (dev - 1) * ells, 0, 3 * ells - 1)]

    def distances(index):
        e, j = near_items[index]
        y = near_source(e, j)[rows : rows + 8] - position_sum[e] * (1.0 / nodes)
        pieces = thirds(y)
        blocks = [pieces[p] for _, p in SPLITS] + [edge(y, 0, 3), jnp.zeros_like(y)]
        split = jnp.concatenate(blocks, axis=0).astype(BF16)
        for chunk in range(0, nodes, ROWS):
            squares[index % 2, chunk : chunk + ROWS, :] = jnp.dot(
                columns[e, chunk : chunk + ROWS, :], split, preferred_element_type=F32
            )

    def near_pair(index):
        e, j = near_items[index]
        slot = index % 2
        for chunk in range(0, nodes, ROWS):
            squared = squares[slot, chunk : chunk + ROWS, :]
            inverse = lax.rsqrt(squared)
            s, c = half_turn(squared * inverse, SIN_TABLE, COS_TABLE)
            scaled = s * inverse
            near_r[slot, chunk : chunk + ROWS, :] = (inverse - s * scaled).astype(BF16)
            near_i[slot, chunk : chunk + ROWS, :] = (scaled * c).astype(BF16)
        values = near_source(e, j)[0:rows]
        near_acc[e] += inward(both(values, near_r[slot], 1), both(values, near_i[slot], 1))

    def near_run(start, stop):
        if start < stop:
            distances(start)
        for index in range(start, stop):
            if index + 1 < stop:
                distances(index + 1)
            near_pair(index)

    early = pairs_total - min(LATE, pairs_total)
    near_run(0, early)

    ready("up_src", "up_op", "up_ops")
    every_parent.wait_recv()

    def coarse(box):
        total = None
        for j in range(up_src.shape[1]):
            term = translate(up_ops, up_op[box, j], gathered[up_src[box, j]])
            total = term if total is None else total + term
        return total

    mine = si * team + member_of_team
    first_box = bi - member_of_team
    team_levels = team // twins if team > 1 else 1

    def hand(source, receive, box, sample):
        pltpu.make_async_remote_copy(
            src_ref=source, dst_ref=full.at[mine], send_sem=local_sem.at[0], recv_sem=recv_sem.at[receive],
            device_id={"box": box, "sample": sample}, device_id_type=MESH,
        ).start()

    def mate(rise, turned):
        return ((member_of_team // twins + rise) % team_levels) * twins + (member_of_team + turned) % twins

    close = [mate(0, turned) for turned in range(1, twins)] if team > 1 else []
    distant = [mate(rise, turned) for rise in range(team_levels - 1, 0, -1) for turned in range(twins)]
    for slot, (to, receive) in enumerate([(to, 5) for to in distant] + [(to, 3) for to in close]):
        cross[slot] = coarse(first_box + to)
        for off in range(ns - 1, -1, -1):
            hand(cross.at[slot], receive, first_box + to, (si + off) % ns)
    full[mine] = coarse(bi)
    hand(full.at[mine], 2, bi, (si + 1) % ns)
    handed = bulk(full.at[pl.ds(0, 1 + ns * (team - 1))], 0, 2)

    near_run(early, pairs_total)

    arrive_b()
    ready("leaf_src", "leaf_op", "leaf_ops")
    incoming = []
    for b in range(boxes):
        total = None
        for j in range(leaf_src.shape[1]):
            source = pat[jnp.clip(leaf_src[b, j] - (dev - 1) * boxes, 0, 3 * boxes - 1)]
            term = translate(leaf_ops, leaf_op[b, j], source)
            total = term if total is None else total + term
        incoming.append(total)


    def lower(slot, t):
        values = full[halves[slot] * team + t]
        lowered = jnp.concatenate(
            [
                inward(values * phases[slot, t, 0, b : b + 1, :], values * phases[slot, t, 1, b : b + 1, :])
                for b in range(boxes)
            ],
            axis=0,
        )
        return both(lowered, interp[slot, t], 1)

    lowered = lower(0, member_of_team)
    bulk(full.at[0], 0, 2).wait_recv()
    lowered = lowered + lower(1, member_of_team)
    for mates, receive in ((close, 3), (distant, 5)):
        if mates:
            bulk(full.at[pl.ds(0, ns * len(mates))], 0, receive).wait_recv()
        for t in mates:
            for slot in range(ns):
                lowered = lowered + lower(slot, t)
    for b in range(boxes):
        incoming[b] = incoming[b] + lowered[b * rows : (b + 1) * rows]

    lane = lax.broadcasted_iota(jnp.int32, (rows, 128), 1)
    row = lax.broadcasted_iota(jnp.int32, (rows, 128), 0)
    square = jnp.zeros((rows, 1), F32)
    straight = [jnp.zeros((rows, 1), F32) for _ in range(vectors)]
    crossed = [jnp.zeros((rows, 1), F32) for _ in range(vectors)]
    for e in range(ells):
        arriving = incoming[0] * member[0][e]
        for b in range(1, boxes):
            arriving = arriving + incoming[b] * member[b][e]
        far = inward(both(arriving, cos_tab[e], 0), both(arriving, sin_tab[e], 0))
        value = ks[vectors - 1, e] + near_acc[e] + far * leaf_width ** (-0.5)
        result[e] = value
        other = swap(value)
        square = square + jnp.sum(value * value, axis=1, keepdims=True)
        for m in range(vectors):
            basis = ks[m, e]
            straight[m] = straight[m] + jnp.sum(basis * value, axis=1, keepdims=True)
            crossed[m] = crossed[m] + jnp.sum(basis * other, axis=1, keepdims=True)
    packed = jnp.where(lane == vectors * rows + row, jnp.broadcast_to(square, lane.shape), 0.0)
    for m in range(vectors):
        a = jnp.broadcast_to(straight[m], lane.shape)
        b = jnp.broadcast_to(crossed[m], lane.shape)
        dots = jnp.where(row < inc, a + swap(a), swap(b) - b)
        packed = packed + jnp.where(lane == m * rows + row, dots, 0.0)
    share_row[...] = jnp.sum(packed, axis=0, keepdims=True)

    def share(box, sample):
        pltpu.make_async_remote_copy(
            src_ref=share_row, dst_ref=sums_hbm.at[dev], send_sem=local_sem.at[10], recv_sem=recv_sem.at[4],
            device_id={"box": box, "sample": sample}, device_id_type=MESH,
        ).start()

    all_others(share)
    outs = [
        pltpu.make_async_copy(share_row, sums_hbm.at[dev], local_sem.at[1]),
        pltpu.make_async_copy(result, result_hbm, local_sem.at[2]),
    ]
    for copy in outs:
        copy.start()
    finish_b()
    handed.wait_send()
    every_parent.wait_send()
    every_sum = bulk(sums_hbm.at[pl.ds(0, nd - 1)], 10, 4)
    every_sum.wait_send()
    for copy in outs:
        copy.wait()
    every_sum.wait_recv()


def finish(sums, result, krylov, h_out, norm_out, next_out):
    _, vectors, ells, inc, nodes = krylov.shape
    rows = 2 * inc
    lane = lax.broadcasted_iota(jnp.int32, (rows, 128), 1)
    row = lax.broadcasted_iota(jnp.int32, (rows, 128), 0)
    sign = jnp.where(lax.broadcasted_iota(jnp.int32, (rows, 1), 0) < inc, 1.0, -1.0)
    total = sums[0]
    for index in range(1, sums.shape[0]):
        total = total + sums[index]
    total = total * (1.0 / (ells * nodes * sums.shape[0]))
    spread = jnp.broadcast_to(total, lane.shape)

    def column(start):
        return jnp.sum(
            jnp.where(lane == start + lax.rem(row, inc), spread, 0.0), axis=1, keepdims=True
        )

    real = [column(m * rows) for m in range(vectors)]
    imag = [column(m * rows + inc) for m in range(vectors)]
    norm_sq = column(vectors * rows) + column(vectors * rows + inc)
    for m in range(vectors):
        norm_sq = norm_sq - (real[m] * real[m] + imag[m] * imag[m])
    norm = jnp.sqrt(norm_sq)
    for m in range(vectors):
        for q in range(2):
            at = m * rows + q * inc
            h_out[q, m : m + 1, :] = total[:, at : at + inc]
    flat = jnp.sum(
        jnp.where((lane == row) & (row < inc), jnp.broadcast_to(norm, lane.shape), 0.0), axis=0, keepdims=True
    )
    norm_out[...] = flat[:, 0:inc]
    for e in range(ells):
        kept = result[e]
        for m in range(vectors):
            basis = jnp.concatenate([krylov[q, m, e] for q in range(2)], axis=0)
            kept = kept - (basis * real[m] - sign * pltpu.roll(basis * imag[m], inc, 0))
        kept = kept / norm
        for q in range(2):
            next_out[q, e] = kept[q * inc : (q + 1) * inc]


def body(
    nb,
    ns,
    krylov,
    self_inv,
    node_pos,
    node_wts,
    box_of,
    near_list,
    leaf_src,
    leaf_op,
    leaf_ops,
    interp,
    parent_centers,
    up_src,
    up_op,
    up_ops,
):
    _, vectors, inc, ells, nodes = krylov.shape
    rows = 2 * inc
    boxes = leaf_src.shape[0]
    leaf_width, up_width = interp.shape
    half = up_ops.shape[2]
    nd = nb * ns
    team = next(size for size in (TEAM, 2, 1) if nb % size == 0)
    part = half // team
    directions = sphere_points(leaf_width).T
    pieces = []
    for _ in range(3):
        pieces.append(directions.astype(BF16))
        directions = directions - pieces[-1].astype(np.float32)
    leaf_dirs = np.zeros((leaf_width, 8 * len(SPLITS)), BF16)
    for block, (piece, _) in enumerate(SPLITS):
        leaf_dirs[:, 8 * block : 8 * block + 3] = pieces[piece]
    up_dirs = np.zeros((ns, 8, half), np.float32)
    up_dirs[:, :3] = np.moveaxis(sphere_points(up_width).reshape(3, ns, half), 1, 0)
    small = [box_of, near_list, leaf_src, leaf_op, up_src, up_op, parent_centers.T]
    large = [jnp.transpose(krylov, (0, 1, 3, 2, 4)), self_inv, node_pos, node_wts]
    large += [jnp.asarray(leaf_dirs), jnp.asarray(up_dirs)]
    vmem = pl.BlockSpec(memory_space=pltpu.VMEM)
    hbm = pl.BlockSpec(memory_space=pl.ANY)
    dma = pltpu.SemaphoreType.DMA
    shapes = (
        jax.ShapeDtypeStruct((2, vectors, inc), F32),
        jax.ShapeDtypeStruct((1, inc), F32),
        jax.ShapeDtypeStruct((2, ells, inc, nodes), F32),
    )
    sums, result = pl.pallas_call(
        functools.partial(kernel, nb, ns),
        out_shape=(
            jax.ShapeDtypeStruct((nd, 1, 128), F32),
            jax.ShapeDtypeStruct((ells, rows, nodes), F32),
        ),
        in_specs=[hbm] * 16,
        out_specs=(hbm, hbm),
        scratch_shapes=[pltpu.SMEM(x.shape, x.dtype) for x in small]
        + [pltpu.VMEM(x.shape, x.dtype) for x in large]
        + [
            pltpu.VMEM(leaf_ops.shape, F32),
            pltpu.VMEM((ns, leaf_width, half), F32),
            pltpu.VMEM((*up_ops.shape[:2], part), F32),
            pltpu.VMEM((ns, team, leaf_width, part), BF16),
            pltpu.VMEM((vectors, ells, rows, nodes), F32),
            pltpu.VMEM((3 * ells, rows + 8, nodes), F32),
            pltpu.VMEM((ns, team, 2, boxes, part), F32),
            pltpu.VMEM((ells, nodes, 8 * len(SPLITS) + 16), BF16),
            pltpu.VMEM((ells, 8 * len(SPLITS), nodes), BF16),
            pltpu.VMEM((ells, leaf_width, nodes), F32),
            pltpu.VMEM((ells, leaf_width, nodes), BF16),
            pltpu.VMEM((ells, leaf_width, nodes), BF16),
            pltpu.VMEM((3 * boxes, rows, leaf_width), F32),
            pltpu.VMEM((team, rows, part), F32),
            pltpu.VMEM((team, rows, part), F32),
            pltpu.VMEM((team, rows, part), F32),
            pltpu.VMEM((nb, rows, part), F32),
            pltpu.VMEM((team, rows, part), F32),
            pltpu.VMEM((ns * team, rows, part), F32),
            pltpu.VMEM((2, nodes, nodes), F32),
            pltpu.VMEM((2, nodes, nodes), BF16),
            pltpu.VMEM((2, nodes, nodes), BF16),
            pltpu.VMEM((ells, rows, nodes), F32),
            pltpu.VMEM((ells, rows, nodes), F32),
            pltpu.VMEM((1, 128), F32),
            dma((11,)),
            dma((2,)),
            dma((2,)),
            dma((6,)),
        ],
        compiler_params=pltpu.CompilerParams(
            collective_id=0, has_side_effects=True, vmem_limit_bytes=67043328
        ),
    )(*small, *large, leaf_ops, interp, up_ops)
    h_column, h_norm, next_vector = pl.pallas_call(
        finish,
        out_shape=shapes,
        in_specs=[vmem] * 3,
        out_specs=(vmem, vmem, vmem),
    )(sums, result, large[0])
    return h_column, h_norm.reshape(inc), jnp.transpose(next_vector, (0, 2, 1, 3))


def solution(mesh):
    placed = (
        P(None, None, None, ("group", "box", "sample"), None),
        P(None, ("group", "box", "sample"), None, None),
        P(None, ("group", "box", "sample"), None),
        P(("group", "box", "sample"), None),
        P(("group", "box", "sample")),
        P(("group", "box", "sample"), None),
        P(("group", "box", "sample"), None),
        P(("group", "box", "sample"), None),
        P(),
        P(),
        P(None, ("group", "box")),
        P("group", None),
        P("group", None),
        P(None, None, "sample"),
    )
    return jax.shard_map(
        functools.partial(body, mesh.shape["box"], mesh.shape["sample"]),
        mesh=mesh,
        in_specs=placed,
        out_specs=(P(None, None, "group"), P("group"), P(None, None, ("box", "sample"), "group")),
        check_vma=False,
    )
```

```python
import functools
import math

import jax
import jax.numpy as jnp
import numpy as np
from jax import lax
from jax.experimental import pallas as pl
from jax.experimental.pallas import tpu as pltpu
from jax.sharding import PartitionSpec as P

MESH = pl.DeviceIdType.MESH
F32 = jnp.float32
BF16 = jnp.bfloat16
ROWS = 64
SPAN = 256
TEAM = 4
LATE = 8
SPLITS = ((0, 0), (1, 0), (2, 0), (0, 1), (1, 1), (0, 2))


def sphere_points(total):
    position = np.arange(total).astype(np.float32)
    height = np.float32(1.0) - (np.float32(2.0) * position + np.float32(1.0)) / np.float32(total)
    radius = np.sqrt(np.float32(1.0) - height * height)
    angle = (position * np.float32(math.pi * (3.0 - math.sqrt(5.0)))).astype(np.float64)
    points = [radius * np.cos(angle).astype(np.float32), radius * np.sin(angle).astype(np.float32), height]
    return np.stack(points).astype(np.float32)


SIN_TABLE = (4.44286798223381, -7.307445412162602, 3.594802094687321, -0.7844036018968589)
COS_TABLE = (1.414204080580398, -6.977642059296966, 5.715238406047747, -1.7283486673722932)
SIN_FULL = (4.442882834891658, -7.308241184631927, 3.6062893308970487, -0.8457654001243101, 0.10920874958601288)
COS_FULL = (1.4142134965660362, -6.978850988281385, 5.739461171112273, -1.88356298861798, 0.31069819238699753)


def series(coefs, u):
    total = coefs[-1]
    for coef in coefs[-2::-1]:
        total = total * u + coef
    return total


def half_turn(t, sin_coefs, cos_coefs):
    f = t - jnp.round(t)
    u = f * f
    return series(sin_coefs, u) * f, series(cos_coefs, u)


def turn(t, sin_coefs=SIN_TABLE, cos_coefs=COS_TABLE):
    s, c = half_turn(t, sin_coefs, cos_coefs)
    return 1.0 - s * s, s * c


def thirds(x):
    high = x.astype(BF16).astype(F32)
    rest = x - high
    middle = rest.astype(BF16).astype(F32)
    return high, middle, rest - middle


def pair(x):
    high = x.astype(BF16).astype(F32)
    return jnp.concatenate([high, x - high], axis=0).astype(BF16)


def both(x, table, contract):
    rows = x.shape[0]
    out = lax.dot_general(
        pair(x), table, (((1,), (contract,)), ((), ())), preferred_element_type=F32
    )
    return out[:rows] + out[rows:]


def kernel(
    box_count_axis,
    sample_count_axis,
    box_of_hbm,
    near_list_hbm,
    leaf_src_hbm,
    leaf_op_hbm,
    up_src_hbm,
    up_op_hbm,
    parent_centers_hbm,
    krylov_hbm,
    self_inv_hbm,
    node_pos_hbm,
    node_wts_hbm,
    leaf_dirs_hbm,
    up_dirs_hbm,
    leaf_ops_hbm,
    interp_hbm,
    up_ops_hbm,
    sums_hbm,
    result_hbm,
    box_of,
    near_list,
    leaf_src,
    leaf_op,
    up_src,
    up_op,
    parent_centers,
    krylov,
    self_inv,
    node_pos,
    node_wts,
    leaf_dirs,
    up_dirs,
    leaf_ops,
    interp_raw,
    up_ops,
    interp,
    ks,
    halo,
    phases,
    columns,
    split_pos,
    turns,
    cos_tab,
    sin_tab,
    pat,
    give,
    take,
    parents,
    gathered,
    cross,
    full,
    squares,
    near_r,
    near_i,
    near_acc,
    result,
    share_row,
    local_sem,
    recv_a,
    recv_b,
    recv_sem,
):
    nb, ns = box_count_axis, sample_count_axis
    nd = nb * ns
    _, vectors, ells, inc, nodes = krylov.shape
    rows = 2 * inc
    boxes = leaf_src.shape[0]
    near_count = near_list.shape[1]
    team, leaf_width, part = interp.shape[1:]
    half = team * part
    pairs_total = ells * near_count
    bi = lax.axis_index("box")
    si = lax.axis_index("sample")
    dev = bi * ns + si
    twins = 2 if nb % 2 == 0 else 1
    levels = nb // twins
    level = bi // twins
    member_of_team = bi % team
    groups = nb // team

    def wrapped(value, size):
        return jnp.where(value >= size, value - size, value)

    own_group = bi // team
    bases = [wrapped(own_group + 1 + g, groups) * team for g in range(groups - 1)] + [own_group * team]
    cores = [si] + [wrapped(si + flip, ns) for flip in range(1, ns)]

    def load(slot, source, target):
        copy = pltpu.make_async_copy(source, target, local_sem.at[slot])
        copy.start()
        return copy

    loads = {}

    def begin(first, **arrays):
        for slot, (name, (source, target)) in enumerate(arrays.items()):
            loads[name] = load(first + slot, source, target)

    def ready(*wanted):
        for name in wanted:
            loads[name].wait()

    def place(index):
        return {"box": index // ns, "sample": index % ns}

    begin(0, box_of=(box_of_hbm, box_of), node_pos=(node_pos_hbm, node_pos), leaf_dirs=(leaf_dirs_hbm, leaf_dirs))
    barrier = pltpu.get_barrier_semaphore()
    shift = 0
    far_first = [wrapped(t + shift, team) for t in range(team)]

    def all_others(act):
        for base in bases[:-1]:
            for t in far_first:
                for core in cores:
                    act(base + t, core)
        for turn_by in range(team):
            for core in cores[1 if turn_by == 0 else 0 :]:
                act(bases[-1] + wrapped(member_of_team + turn_by, team), core)

    all_others(
        lambda box, core: pl.semaphore_signal(
            barrier, inc=1, device_id={"box": box, "sample": core}, device_id_type=MESH
        )
    )
    begin(
        3, krylov=(krylov_hbm, krylov), node_wts=(node_wts_hbm, node_wts), self_inv=(self_inv_hbm, self_inv),
        parent_centers=(parent_centers_hbm, parent_centers), up_dirs=(up_dirs_hbm, up_dirs),
    )
    halves = cores[:2]

    def begin_interp(slot):
        at = pl.ds(pl.multiple_of(halves[slot] * half, half), half)
        loads["interp", slot] = load(9 - slot, interp_hbm.at[:, at], interp_raw.at[slot])

    begin_interp(1)

    sign = jnp.where(lax.broadcasted_iota(jnp.int32, (rows, 1), 0) < inc, 1.0, -1.0)

    def swap(x):
        return pltpu.roll(x, inc, 0)

    def inward(c, d):
        return c - sign * swap(d)

    def outward(c, d):
        return c + sign * swap(d)

    def neighbours(buffer, width, send, recv):
        own = buffer.at[pl.ds(width, width)]
        right = pltpu.make_async_remote_copy(
            src_ref=own, dst_ref=buffer.at[pl.ds(0, width)], send_sem=local_sem.at[send], recv_sem=recv.at[0],
            device_id=place((dev + 1) % nd), device_id_type=MESH,
        )
        left = pltpu.make_async_remote_copy(
            src_ref=own, dst_ref=buffer.at[pl.ds(2 * width, width)], send_sem=local_sem.at[send + 1], recv_sem=recv.at[1],
            device_id=place((dev + nd - 1) % nd), device_id_type=MESH,
        )

        def start():
            @pl.when((si == 0) & (dev > 0))
            def _():
                left.start()

            @pl.when(dev < nd - 1)
            def _():
                right.start()

            @pl.when(si > 0)
            def _():
                left.start()

        def arrive():
            @pl.when(dev > 0)
            def _():
                right.wait_recv()

            @pl.when(dev < nd - 1)
            def _():
                left.wait_recv()

        def finish():
            @pl.when(dev < nd - 1)
            def _():
                right.wait_send()

            @pl.when(dev > 0)
            def _():
                left.wait_send()

        return start, arrive, finish

    start_a, arrive_a, finish_a = neighbours(halo, ells, 7, recv_a)
    start_b, arrive_b, finish_b = neighbours(pat, boxes, 7, recv_b)

    ready("node_pos", "box_of")
    for e in range(ells):
        for axis in range(3):
            halo[ells + e, rows + axis : rows + axis + 1, :] = node_pos[axis, e : e + 1, :]
        halo[ells + e, rows + 3 :, :] = jnp.zeros((halo.shape[1] - rows - 3, nodes), F32)

    member = [
        [jnp.where(box_of[e] - dev * boxes == b, 1.0, 0.0) for e in range(ells)] for b in range(boxes)
    ]
    position_sum = [
        jnp.sum(halo[ells + e, rows : rows + 8, :], axis=1, keepdims=True) for e in range(ells)
    ]
    centers = []
    for b in range(boxes):
        total = position_sum[0] * member[b][0]
        amount = member[b][0]
        for e in range(1, ells):
            total = total + position_sum[e] * member[b][e]
            amount = amount + member[b][e]
        centers.append(total / (jnp.full((8, 1), 1.0, F32) * (amount * nodes)))
    for e in range(ells):
        middle = centers[0] * member[0][e]
        for b in range(1, boxes):
            middle = middle + centers[b] * member[b][e]
        here = halo[ells + e, rows : rows + 8, :]
        pieces = thirds(here - middle)
        split_pos[e] = jnp.concatenate([pieces[p] for _, p in SPLITS], axis=0).astype(BF16)

    nt = (((1,), (1,)), ((), ()))
    spans = [pl.ds(start, SPAN) for start in range(0, leaf_width, SPAN)]

    def angles(e, span):
        turns[e, span, :] = jnp.dot(leaf_dirs[span, :], split_pos[e], preferred_element_type=F32)

    def fill(e, span):
        cosine, sine = turn(turns[e, span, :])
        cos_tab[e, span, :] = cosine.astype(BF16)
        sin_tab[e, span, :] = sine.astype(BF16)

    def gather_up(e, span):
        c = lax.dot_general(pairs[e], cos_tab[e, span, :], nt, preferred_element_type=F32)
        d = lax.dot_general(pairs[e], sin_tab[e, span, :], nt, preferred_element_type=F32)
        piece = outward(c[:rows] + c[rows:], d[:rows] + d[rows:])
        for b in range(boxes):
            part = piece * member[b][e]
            pat[boxes + b, :, span] = part if e == 0 else pat[boxes + b, :, span] + part

    ready("leaf_dirs")
    for span in spans:
        angles(0, span)
    for span in spans:
        if ells > 1:
            angles(1, span)
        fill(0, span)

    ready("krylov", "node_wts", "self_inv", "parent_centers", "up_dirs")
    begin_interp(0)
    begin(
        0, near_list=(near_list_hbm, near_list), leaf_src=(leaf_src_hbm, leaf_src), leaf_op=(leaf_op_hbm, leaf_op),
        up_src=(up_src_hbm, up_src), up_op=(up_op_hbm, up_op),
        up_ops=(up_ops_hbm.at[:, :, pl.ds(pl.multiple_of(member_of_team * part, part), part)], up_ops),
        leaf_ops=(leaf_ops_hbm, leaf_ops),
    )
    pairs = []
    for e in range(ells):
        rounded = jnp.concatenate([krylov[q, vectors - 1, e] for q in range(2)], axis=0).astype(BF16)
        c = lax.dot_general(rounded, self_inv[0, e], nt, preferred_element_type=F32)
        d = lax.dot_general(rounded, self_inv[1, e], nt, preferred_element_type=F32)
        source = inward(c, d) * node_wts[e : e + 1, :]
        halo[ells + e, 0:rows, :] = source
        pairs.append(pair(source))


    def up_phase(center, dirs):
        t = (center[0:1] - parent_centers[0, 0]) * dirs[0:1]
        for axis in range(1, 3):
            t = t + (center[axis : axis + 1] - parent_centers[0, axis]) * dirs[axis : axis + 1]
        return t

    def turns_of(list_of_centers, dirs):
        t = jnp.concatenate([up_phase(center, dirs) for center in list_of_centers], axis=0)
        return turn(t, SIN_FULL, COS_FULL)

    for slot, h in enumerate(halves):
        cosine, sine = turns_of(centers, up_dirs[h])
        for t in range(team):
            phases[slot, t, 0] = cosine[:, t * part : (t + 1) * part]
            phases[slot, t, 1] = sine[:, t * part : (t + 1) * part]

    pending = [(0, span) for span in spans] if ells > 1 else []
    for e in range(min(1, ells - 1), ells):
        for span in spans:
            if e + 1 < ells:
                angles(e + 1, span)
            if e > 0:
                fill(e, span)
            for _ in range(min(len(pending), 2 if e > 1 else 1)):
                gather_up(*pending.pop(0))
            pending.append((e, span))
    for item in pending:
        gather_up(*item)

    whole = pair(jnp.concatenate([pat[boxes + b] for b in range(boxes)], axis=0))

    def lift(slot, t):
        table = interp_raw[slot, :, t * part : (t + 1) * part].astype(BF16)
        interp[slot, t] = table
        lifted = jnp.dot(whole, table, preferred_element_type=F32)
        lifted = lifted[: boxes * rows] + lifted[boxes * rows :]
        parent = None
        for b in range(boxes):
            piece = lifted[b * rows : (b + 1) * rows]
            term = outward(
                piece * phases[slot, t, 0, b : b + 1, :], piece * phases[slot, t, 1, b : b + 1, :]
            )
            parent = term if parent is None else parent + term
        return parent

    partner_id = {"box": bi, "sample": cores[1]}

    def swap_part(t):
        return pltpu.make_async_remote_copy(
            src_ref=give.at[t], dst_ref=take.at[t], send_sem=local_sem.at[10], recv_sem=recv_sem.at[0],
            device_id=partner_id, device_id_type=MESH,
        )

    def bulk(ref, send, receive):
        return pltpu.make_async_remote_copy(
            src_ref=ref, dst_ref=ref, send_sem=local_sem.at[send], recv_sem=recv_sem.at[receive],
            device_id=partner_id, device_id_type=MESH,
        )

    def deliver(box, t):
        pltpu.make_async_remote_copy(
            src_ref=parents.at[t], dst_ref=gathered.at[bi], send_sem=local_sem.at[9],
            recv_sem=recv_sem.at[1], device_id={"box": box, "sample": si}, device_id_type=MESH,
        ).start()

    ready(("interp", 1))
    for t in range(team):
        give[t] = lift(1, t)
    pl.semaphore_wait(barrier, nd - 1)
    for t in range(team):
        swap_part(t).start()
    start_a()
    ready(("interp", 0))
    own_part = [lift(0, t) for t in range(team)]
    def edge(x, first, ones):
        parts = thirds(jnp.sum(x * x, axis=0, keepdims=True))
        at = lax.broadcasted_iota(jnp.int32, x.shape, 0)
        block = jnp.where((at >= ones) & (at < ones + 3), 1.0, 0.0)
        for p in range(3):
            block = jnp.where(at == first + p, jnp.broadcast_to(parts[p], x.shape), block)
        return block

    for e in range(ells):
        x = halo[ells + e, rows : rows + 8, :] - position_sum[e] * (1.0 / nodes)
        pieces = thirds(-2.0 * x)
        blocks = [pieces[p] for p, _ in SPLITS] + [edge(x, 3, 0)]
        blocks.append(jnp.zeros_like(x))
        columns[e] = jnp.transpose(jnp.concatenate(blocks, axis=0)).astype(BF16)
        for m in range(vectors):
            for q in range(2):
                ks[m, e, q * inc : (q + 1) * inc, :] = krylov[q, m, e]

    swapped = bulk(full.at[pl.ds(0, team)], 10, 0)
    swapped.wait_recv()
    for t in range(team):
        parents[t] = own_part[t] + take[t]
    for t in range(team):
        for base in bases[:-1]:
            deliver(base + t, t)

        @pl.when(member_of_team != t)
        def _(t=t):
            deliver(bases[-1] + t, t)

    every_parent = bulk(gathered.at[pl.ds(0, nb - 1)], 9, 1)
    gathered[bi] = parents[member_of_team]
    swapped.wait_send()
    finish_a()
    start_b()

    def translate(operators, index, values):
        pair_rows = operators[index]
        return inward(values * pair_rows[0:1], values * pair_rows[1:2])

    ready("near_list")
    arrive_a()
    near_acc[...] = jnp.zeros(near_acc.shape, F32)

    near_items = [(e, j) for e in range(ells) for j in range(near_count)]

    def near_source(e, j):
        return halo[jnp.clip(near_list[e, j] - (dev - 1) * ells, 0, 3 * ells - 1)]

    def distances(index):
        e, j = near_items[index]
        y = near_source(e, j)[rows : rows + 8] - position_sum[e] * (1.0 / nodes)
        pieces = thirds(y)
        blocks = [pieces[p] for _, p in SPLITS] + [edge(y, 0, 3), jnp.zeros_like(y)]
        split = jnp.concatenate(blocks, axis=0).astype(BF16)
        for chunk in range(0, nodes, ROWS):
            squares[index % 2, chunk : chunk + ROWS, :] = jnp.dot(
                columns[e, chunk : chunk + ROWS, :], split, preferred_element_type=F32
            )

    def near_pair(index):
        e, j = near_items[index]
        slot = index % 2
        for chunk in range(0, nodes, ROWS):
            squared = squares[slot, chunk : chunk + ROWS, :]
            inverse = lax.rsqrt(squared)
            s, c = half_turn(squared * inverse, SIN_TABLE, COS_TABLE)
            scaled = s * inverse
            near_r[slot, chunk : chunk + ROWS, :] = (inverse - s * scaled).astype(BF16)
            near_i[slot, chunk : chunk + ROWS, :] = (scaled * c).astype(BF16)
        values = near_source(e, j)[0:rows]
        near_acc[e] += inward(both(values, near_r[slot], 1), both(values, near_i[slot], 1))

    def near_run(start, stop):
        if start < stop:
            distances(start)
        for index in range(start, stop):
            if index + 1 < stop:
                distances(index + 1)
            near_pair(index)

    early = pairs_total - min(LATE, pairs_total)
    near_run(0, early)

    ready("up_src", "up_op", "up_ops")
    every_parent.wait_recv()

    def coarse(box):
        total = None
        for j in range(up_src.shape[1]):
            term = translate(up_ops, up_op[box, j], gathered[up_src[box, j]])
            total = term if total is None else total + term
        return total

    mine = si * team + member_of_team
    first_box = bi - member_of_team
    team_levels = team // twins if team > 1 else 1

    def hand(source, receive, box, sample):
        pltpu.make_async_remote_copy(
            src_ref=source, dst_ref=full.at[mine], send_sem=local_sem.at[0], recv_sem=recv_sem.at[receive],
            device_id={"box": box, "sample": sample}, device_id_type=MESH,
        ).start()

    def mate(rise, turned):
        return ((member_of_team // twins + rise) % team_levels) * twins + (member_of_team + turned) % twins

    close = [mate(0, turned) for turned in range(1, twins)] if team > 1 else []
    distant = [mate(rise, turned) for rise in range(team_levels - 1, 0, -1) for turned in range(twins)]
    for slot, (to, receive) in enumerate([(to, 5) for to in distant] + [(to, 3) for to in close]):
        cross[slot] = coarse(first_box + to)
        for off in range(ns - 1, -1, -1):
            hand(cross.at[slot], receive, first_box + to, (si + off) % ns)
    full[mine] = coarse(bi)
    hand(full.at[mine], 2, bi, (si + 1) % ns)
    handed = bulk(full.at[pl.ds(0, 1 + ns * (team - 1))], 0, 2)

    near_run(early, pairs_total)

    arrive_b()
    ready("leaf_src", "leaf_op", "leaf_ops")
    incoming = []
    for b in range(boxes):
        total = None
        for j in range(leaf_src.shape[1]):
            source = pat[jnp.clip(leaf_src[b, j] - (dev - 1) * boxes, 0, 3 * boxes - 1)]
            term = translate(leaf_ops, leaf_op[b, j], source)
            total = term if total is None else total + term
        incoming.append(total)


    def lower(slot, t):
        values = full[halves[slot] * team + t]
        lowered = jnp.concatenate(
            [
                inward(values * phases[slot, t, 0, b : b + 1, :], values * phases[slot, t, 1, b : b + 1, :])
                for b in range(boxes)
            ],
            axis=0,
        )
        return both(lowered, interp[slot, t], 1)

    lowered = lower(0, member_of_team)
    bulk(full.at[0], 0, 2).wait_recv()
    lowered = lowered + lower(1, member_of_team)
    for mates, receive in ((close, 3), (distant, 5)):
        if mates:
            bulk(full.at[pl.ds(0, ns * len(mates))], 0, receive).wait_recv()
        for t in mates:
            for slot in range(ns):
                lowered = lowered + lower(slot, t)
    for b in range(boxes):
        incoming[b] = incoming[b] + lowered[b * rows : (b + 1) * rows]

    lane = lax.broadcasted_iota(jnp.int32, (rows, 128), 1)
    row = lax.broadcasted_iota(jnp.int32, (rows, 128), 0)
    square = jnp.zeros((rows, 1), F32)
    straight = [jnp.zeros((rows, 1), F32) for _ in range(vectors)]
    crossed = [jnp.zeros((rows, 1), F32) for _ in range(vectors)]
    for e in range(ells):
        arriving = incoming[0] * member[0][e]
        for b in range(1, boxes):
            arriving = arriving + incoming[b] * member[b][e]
        far = inward(both(arriving, cos_tab[e], 0), both(arriving, sin_tab[e], 0))
        value = ks[vectors - 1, e] + near_acc[e] + far * leaf_width ** (-0.5)
        result[e] = value
        other = swap(value)
        square = square + jnp.sum(value * value, axis=1, keepdims=True)
        for m in range(vectors):
            basis = ks[m, e]
            straight[m] = straight[m] + jnp.sum(basis * value, axis=1, keepdims=True)
            crossed[m] = crossed[m] + jnp.sum(basis * other, axis=1, keepdims=True)
    packed = jnp.where(lane == vectors * rows + row, jnp.broadcast_to(square, lane.shape), 0.0)
    for m in range(vectors):
        a = jnp.broadcast_to(straight[m], lane.shape)
        b = jnp.broadcast_to(crossed[m], lane.shape)
        dots = jnp.where(row < inc, a + swap(a), swap(b) - b)
        packed = packed + jnp.where(lane == m * rows + row, dots, 0.0)
    share_row[...] = jnp.sum(packed, axis=0, keepdims=True)

    def share(box, sample):
        pltpu.make_async_remote_copy(
            src_ref=share_row, dst_ref=sums_hbm.at[dev], send_sem=local_sem.at[10], recv_sem=recv_sem.at[4],
            device_id={"box": box, "sample": sample}, device_id_type=MESH,
        ).start()

    all_others(share)
    outs = [
        pltpu.make_async_copy(share_row, sums_hbm.at[dev], local_sem.at[1]),
        pltpu.make_async_copy(result, result_hbm, local_sem.at[2]),
    ]
    for copy in outs:
        copy.start()
    finish_b()
    handed.wait_send()
    every_parent.wait_send()
    every_sum = bulk(sums_hbm.at[pl.ds(0, nd - 1)], 10, 4)
    every_sum.wait_send()
    for copy in outs:
        copy.wait()
    every_sum.wait_recv()


def finish(sums, result, krylov, h_out, norm_out, next_out):
    _, vectors, ells, inc, nodes = krylov.shape
    rows = 2 * inc
    lane = lax.broadcasted_iota(jnp.int32, (rows, 128), 1)
    row = lax.broadcasted_iota(jnp.int32, (rows, 128), 0)
    sign = jnp.where(lax.broadcasted_iota(jnp.int32, (rows, 1), 0) < inc, 1.0, -1.0)
    total = sums[0]
    for index in range(1, sums.shape[0]):
        total = total + sums[index]
    total = total * (1.0 / (ells * nodes * sums.shape[0]))
    spread = jnp.broadcast_to(total, lane.shape)

    def column(start):
        return jnp.sum(
            jnp.where(lane == start + lax.rem(row, inc), spread, 0.0), axis=1, keepdims=True
        )

    real = [column(m * rows) for m in range(vectors)]
    imag = [column(m * rows + inc) for m in range(vectors)]
    norm_sq = column(vectors * rows) + column(vectors * rows + inc)
    for m in range(vectors):
        norm_sq = norm_sq - (real[m] * real[m] + imag[m] * imag[m])
    norm = jnp.sqrt(norm_sq)
    for m in range(vectors):
        for q in range(2):
            at = m * rows + q * inc
            h_out[q, m : m + 1, :] = total[:, at : at + inc]
    flat = jnp.sum(
        jnp.where((lane == row) & (row < inc), jnp.broadcast_to(norm, lane.shape), 0.0), axis=0, keepdims=True
    )
    norm_out[...] = flat[:, 0:inc]
    for e in range(ells):
        kept = result[e]
        for m in range(vectors):
            basis = jnp.concatenate([krylov[q, m, e] for q in range(2)], axis=0)
            kept = kept - (basis * real[m] - sign * pltpu.roll(basis * imag[m], inc, 0))
        kept = kept / norm
        for q in range(2):
            next_out[q, e] = kept[q * inc : (q + 1) * inc]


def body(
    nb,
    ns,
    krylov,
    self_inv,
    node_pos,
    node_wts,
    box_of,
    near_list,
    leaf_src,
    leaf_op,
    leaf_ops,
    interp,
    parent_centers,
    up_src,
    up_op,
    up_ops,
):
    _, vectors, inc, ells, nodes = krylov.shape
    rows = 2 * inc
    boxes = leaf_src.shape[0]
    leaf_width, up_width = interp.shape
    half = up_ops.shape[2]
    nd = nb * ns
    team = next(size for size in (TEAM, 2, 1) if nb % size == 0)
    part = half // team
    directions = sphere_points(leaf_width).T
    pieces = []
    for _ in range(3):
        pieces.append(directions.astype(BF16))
        directions = directions - pieces[-1].astype(np.float32)
    leaf_dirs = np.zeros((leaf_width, 8 * len(SPLITS)), BF16)
    for block, (piece, _) in enumerate(SPLITS):
        leaf_dirs[:, 8 * block : 8 * block + 3] = pieces[piece]
    up_dirs = np.zeros((ns, 8, half), np.float32)
    up_dirs[:, :3] = np.moveaxis(sphere_points(up_width).reshape(3, ns, half), 1, 0)
    small = [box_of, near_list, leaf_src, leaf_op, up_src, up_op, parent_centers.T]
    large = [jnp.transpose(krylov, (0, 1, 3, 2, 4)), self_inv, node_pos, node_wts]
    large += [jnp.asarray(leaf_dirs), jnp.asarray(up_dirs)]
    vmem = pl.BlockSpec(memory_space=pltpu.VMEM)
    hbm = pl.BlockSpec(memory_space=pl.ANY)
    dma = pltpu.SemaphoreType.DMA
    shapes = (
        jax.ShapeDtypeStruct((2, vectors, inc), F32),
        jax.ShapeDtypeStruct((1, inc), F32),
        jax.ShapeDtypeStruct((2, ells, inc, nodes), F32),
    )
    sums, result = pl.pallas_call(
        functools.partial(kernel, nb, ns),
        out_shape=(
            jax.ShapeDtypeStruct((nd, 1, 128), F32),
            jax.ShapeDtypeStruct((ells, rows, nodes), F32),
        ),
        in_specs=[hbm] * 16,
        out_specs=(hbm, hbm),
        scratch_shapes=[pltpu.SMEM(x.shape, x.dtype) for x in small]
        + [pltpu.VMEM(x.shape, x.dtype) for x in large]
        + [
            pltpu.VMEM(leaf_ops.shape, F32),
            pltpu.VMEM((ns, leaf_width, half), F32),
            pltpu.VMEM((*up_ops.shape[:2], part), F32),
            pltpu.VMEM((ns, team, leaf_width, part), BF16),
            pltpu.VMEM((vectors, ells, rows, nodes), F32),
            pltpu.VMEM((3 * ells, rows + 8, nodes), F32),
            pltpu.VMEM((ns, team, 2, boxes, part), F32),
            pltpu.VMEM((ells, nodes, 8 * len(SPLITS) + 16), BF16),
            pltpu.VMEM((ells, 8 * len(SPLITS), nodes), BF16),
            pltpu.VMEM((ells, leaf_width, nodes), F32),
            pltpu.VMEM((ells, leaf_width, nodes), BF16),
            pltpu.VMEM((ells, leaf_width, nodes), BF16),
            pltpu.VMEM((3 * boxes, rows, leaf_width), F32),
            pltpu.VMEM((team, rows, part), F32),
            pltpu.VMEM((team, rows, part), F32),
            pltpu.VMEM((team, rows, part), F32),
            pltpu.VMEM((nb, rows, part), F32),
            pltpu.VMEM((team, rows, part), F32),
            pltpu.VMEM((ns * team, rows, part), F32),
            pltpu.VMEM((2, nodes, nodes), F32),
            pltpu.VMEM((2, nodes, nodes), BF16),
            pltpu.VMEM((2, nodes, nodes), BF16),
            pltpu.VMEM((ells, rows, nodes), F32),
            pltpu.VMEM((ells, rows, nodes), F32),
            pltpu.VMEM((1, 128), F32),
            dma((11,)),
            dma((2,)),
            dma((2,)),
            dma((6,)),
        ],
        compiler_params=pltpu.CompilerParams(
            collective_id=0, has_side_effects=True, vmem_limit_bytes=67043328
        ),
    )(*small, *large, leaf_ops, interp, up_ops)
    h_column, h_norm, next_vector = pl.pallas_call(
        finish,
        out_shape=shapes,
        in_specs=[vmem] * 3,
        out_specs=(vmem, vmem, vmem),
    )(sums, result, large[0])
    return h_column, h_norm.reshape(inc), jnp.transpose(next_vector, (0, 2, 1, 3))


def solution(mesh):
    placed = (
        P(None, None, None, ("group", "box", "sample"), None),
        P(None, ("group", "box", "sample"), None, None),
        P(None, ("group", "box", "sample"), None),
        P(("group", "box", "sample"), None),
        P(("group", "box", "sample")),
        P(("group", "box", "sample"), None),
        P(("group", "box", "sample"), None),
        P(("group", "box", "sample"), None),
        P(),
        P(),
        P(None, ("group", "box")),
        P("group", None),
        P("group", None),
        P(None, None, "sample"),
    )
    return jax.shard_map(
        functools.partial(body, mesh.shape["box"], mesh.shape["sample"]),
        mesh=mesh,
        in_specs=placed,
        out_specs=(P(None, None, "group"), P("group"), P(None, None, ("box", "sample"), "group")),
        check_vma=False,
    )
```
